32 devices in a mesh: leaf: 16 (over z, y, x), col: 2 (over core).
Axes of the slice: x: 2, y: 2, z: 4, core: 2. Of those that a mesh axis runs over, the one named last changes fastest.
Arguments:
- sources: bfloat16 [65536, 256], P('leaf', 'col'), may hold values from -6 to 6
- near_tiles: bfloat16 [256, 8, 256, 256], P('leaf', 'col'), may hold values from -0.125 to 0.125
- near_index: int32 [256, 8], P('leaf'), may hold values from 0 to 255, as said below
- near_count: int32 [256], P('leaf'), may hold values from 1 to 8, as said below
- leaf_basis: bfloat16 [256, 64, 256], P('leaf'), may hold values from -0.375 to 0.375
- leaf_coupling: bfloat16 [256, 64, 256], P('leaf'), may hold values from -0.375 to 0.375
- leaf_far: int32 [256, 4], P('leaf'), may hold values from 0 to 255, as said below
- up_leaf: bfloat16 [32, 64, 512], P('leaf'), may hold values from -0.25 to 0.25
- mid_coupling: bfloat16 [32, 64, 256], P('leaf'), may hold values from -0.375 to 0.375
- mid_far: int32 [32, 4], P('leaf'), may hold values from 0 to 31, as said below
- up_mid: bfloat16 [32, 64, 64], P('leaf'), may hold values from -0.75 to 0.75
- top_coupling: bfloat16 [4, 64, 256], replicated, may hold values from -0.4375 to 0.4375
Outputs:
- product: float32 [65536, 256], P('leaf', 'col')
The draws below stay inside these ranges and needn't reach their ends.
Inputs may be any that keep to these rules, and one draw needn't show every extreme that they name: `near_index`: entry 0 of row i is i; the other 7 entries are distinct leaves j with j != i and |i - j| <= 8. Only the first near_count[i] slots of leaf i count; some leaf has all 8. `leaf_far`: row i holds 4 distinct leaves j != i with |i // 8 - j // 8| <= 1. `mid_far`: row a holds 4 distinct middle clusters b != a with |a // 8 - b // 8| <= 1.
All inputs are finite; a program needn't handle non-finite values.
Results may differ from the reference program's by a relative error of at most 0.01.
Values may be sent and summed in bfloat16 or wider, within the bound.
No kernel may reach another device: no remote copies, remote signals or barrier semaphores. Data moves between devices by JAX's collectives and lax.ppermute only.
A program may use at most 128 MiB of HBM per device.

```python
import jax
import jax.numpy as jnp
from jax import lax

LEAF = 256
RANK = 64
COLS = 256
CHILD = 8
NEAR = 8
FAR = 4
LEAVES_DEV = 16
NL = 256
NL1 = 32
NL2 = 4
N = 65536


def window_pick(seed_key, row_count, slot_count, near_only):
    span = 2 * CHILD - 1
    offsets = jnp.arange(-span, span + 1, dtype=jnp.int32)
    rows_ids = jnp.arange(row_count, dtype=jnp.int32)[:, None]
    target = rows_ids + offsets[None, :]
    inside = (target >= 0) & (target < row_count) & (offsets[None, :] != 0)
    if near_only:
        inside = inside & (jnp.abs(offsets)[None, :] <= CHILD)
    else:
        inside = inside & (jnp.abs(rows_ids // CHILD - target // CHILD) <= 1)
    scores = jax.random.randint(seed_key, target.shape, 0, 1 << 20, dtype=jnp.int32) * 64 + jnp.arange(offsets.shape[0], dtype=jnp.int32)[None, :]
    scores = jnp.where(inside, scores, -1)
    _, chosen = lax.top_k(scores, slot_count)
    return jnp.take_along_axis(target, chosen, axis=1).astype(jnp.int32)


def draw_near_index(key, part):
    picked = window_pick(jax.random.fold_in(key, 11), NL, NEAR - 1, True)
    itself = jnp.arange(NL, dtype=jnp.int32)[:, None]
    return jnp.concatenate([itself, picked], axis=1).astype(jnp.int32)


def draw_near_count(key, part):
    device_level = jax.random.randint(jax.random.fold_in(key, 12), (NL // LEAVES_DEV,), 1, NEAR + 1, dtype=jnp.int32)
    jitter = jax.random.randint(jax.random.fold_in(key, 13), (NL,), -1, 2, dtype=jnp.int32)
    counts = jnp.clip(jnp.repeat(device_level, LEAVES_DEV) + jitter, 1, NEAR)
    fullest = jax.random.randint(jax.random.fold_in(key, 14), (), 0, NL, dtype=jnp.int32)
    return counts.at[fullest].set(NEAR).astype(jnp.int32)


def draw_leaf_far(key, part):
    return window_pick(jax.random.fold_in(key, 15), NL, FAR, False)


def draw_mid_far(key, part):
    return window_pick(jax.random.fold_in(key, 16), NL1, FAR, False)


def block_levels(own_key, shape, pieces, smallest, high):
    level = 1.0
    for axis_at, blocks in pieces:
        draws = jax.random.uniform(jax.random.fold_in(jax.random.fold_in(own_key, 6), axis_at), (blocks,), jnp.float32, smallest / len(pieces), high / len(pieces))
        level = level * jnp.repeat(jnp.exp(draws), shape[axis_at] // blocks).reshape((-1,) + (1,) * (len(shape) - 1 - axis_at))
    return level


def bell_draw(stream_key, shape, deviation, most, cuts=(), held_as=jnp.bfloat16):
    entries = deviation * jax.random.normal(stream_key, shape, jnp.float32)
    if cuts:
        entries = entries * block_levels(stream_key, shape, cuts, -0.22, 0.18)
    return jnp.clip(entries, -most, most).astype(held_as)


def setup_inputs(seed: int = 0) -> dict:
    key_of = jax.random.split(jax.random.key(seed), 13)
    sources = bell_draw(key_of[0], (N, COLS), 1.0, 6.0, ((0, 16), (1, 2)))
    near_tiles = bell_draw(key_of[1], (NL, NEAR, LEAF, LEAF), (LEAF * NEAR) ** -0.5, 0.125, ((0, 16), (1, 2)))
    near_index = draw_near_index(jax.random.fold_in(key_of[12], 71), 0)
    near_count = draw_near_count(jax.random.fold_in(key_of[12], 71), 0)
    leaf_basis = bell_draw(key_of[4], (NL, RANK, LEAF), LEAF ** -0.5, 0.375, ((0, 16),))
    leaf_coupling = bell_draw(key_of[5], (NL, RANK, FAR * RANK), (FAR * RANK) ** -0.5, 0.375, ((0, 16),))
    leaf_far = draw_leaf_far(jax.random.fold_in(key_of[12], 71), 0)
    up_leaf = bell_draw(key_of[7], (NL1, RANK, CHILD * RANK), (CHILD * RANK) ** -0.5, 0.25, ((0, 16),))
    mid_coupling = bell_draw(key_of[8], (NL1, RANK, FAR * RANK), (FAR * RANK) ** -0.5, 0.375, ((0, 16),))
    mid_far = draw_mid_far(jax.random.fold_in(key_of[12], 71), 0)
    up_mid = bell_draw(key_of[10], (NL1, RANK, RANK), RANK ** -0.5, 0.75, ((0, 16),))
    top_coupling = bell_draw(key_of[11], (NL2, RANK, NL2 * RANK), ((NL2 - 1) * RANK) ** -0.5, 0.4375)
    return dict(sources=sources, near_tiles=near_tiles, near_index=near_index, near_count=near_count, leaf_basis=leaf_basis, leaf_coupling=leaf_coupling, leaf_far=leaf_far, up_leaf=up_leaf, mid_coupling=mid_coupling, mid_far=mid_far, up_mid=up_mid, top_coupling=top_coupling)


def reference(sources, near_tiles, near_index, near_count, leaf_basis, leaf_coupling, leaf_far, up_leaf, mid_coupling, mid_far, up_mid, top_coupling):
    f32 = jnp.float32
    bf16 = jnp.bfloat16
    blocks = sources.astype(f32).reshape(NL, LEAF, COLS)
    leaf_coef = jnp.einsum("lrk,lkc->lrc", leaf_basis.astype(f32), blocks).astype(bf16)
    mid_coef = jnp.einsum("qrk,qkc->qrc", up_leaf.astype(f32), leaf_coef.astype(f32).reshape(NL1, CHILD * RANK, COLS)).astype(bf16)
    mid_lift = jnp.einsum("qrs,qsc->qrc", up_mid.astype(f32), mid_coef.astype(f32)).astype(bf16)
    top_sum = jnp.sum(mid_lift.astype(f32).reshape(NL2, CHILD, RANK, COLS), axis=1)
    top_coef = top_sum.astype(bf16)
    top_ids = jnp.arange(NL2)
    keep_mask = top_ids[:, None] != top_ids[None, :]
    stacked = jnp.where(keep_mask[:, :, None, None], top_coef.astype(f32)[None], jnp.zeros((), f32))
    top_field = jnp.einsum("prk,pkc->prc", top_coupling.astype(f32), stacked.reshape(NL2, NL2 * RANK, COLS)).astype(bf16)
    mid_picked = mid_coef.astype(f32)[mid_far].reshape(NL1, FAR * RANK, COLS)
    mid_parent = jnp.arange(NL1) // CHILD
    mid_field = (jnp.einsum("qrk,qkc->qrc", mid_coupling.astype(f32), mid_picked)
                 + jnp.einsum("qrs,qrc->qsc", up_mid.astype(f32), top_field.astype(f32)[mid_parent])).astype(bf16)
    leaf_picked = leaf_coef.astype(f32)[leaf_far].reshape(NL, FAR * RANK, COLS)
    down_part = jnp.einsum("qrs,qrc->qsc", up_leaf.astype(f32), mid_field.astype(f32)).reshape(NL, RANK, COLS)
    leaf_field = (jnp.einsum("lrk,lkc->lrc", leaf_coupling.astype(f32), leaf_picked) + down_part).astype(bf16)
    far_part = jnp.einsum("lrk,lrc->lkc", leaf_basis.astype(f32), leaf_field.astype(f32)).reshape(N, COLS)

    def per_leaf(inputs):
        tile_set, index_row, live_count = inputs
        picked = blocks[index_row]
        live_mask = jnp.arange(NEAR) < live_count
        picked = jnp.where(live_mask[:, None, None], picked, jnp.zeros((), f32))
        return jnp.einsum("sij,sjc->ic", tile_set.astype(f32), picked)

    near_part = lax.map(per_leaf, (near_tiles, near_index, near_count)).reshape(N, COLS)
    return near_part + far_part
```

```python
import functools

import jax
import jax.numpy as jnp
from jax import lax
from jax.experimental import pallas as pl
from jax.experimental.pallas import tpu as pltpu
from jax.sharding import PartitionSpec as P

CHILD = 8
FAR = 4
RING = 8

F32 = jnp.float32
BF16 = jnp.bfloat16
VMEM = pl.BlockSpec(memory_space=pltpu.VMEM)
SMEM = pl.BlockSpec(memory_space=pltpu.SMEM)
ANY = pl.BlockSpec(memory_space=pl.ANY)


def mm(a, b):
    return jnp.dot(a, b, preferred_element_type=F32)


def mm_t(a, b):
    return lax.dot_general(a, b, (((0,), (0,)), ((), ())), preferred_element_type=F32)


def cost(flops, nbytes):
    return pl.CostEstimate(flops=flops, transcendentals=0, bytes_accessed=nbytes)


def params(mib):
    return pltpu.CompilerParams(vmem_limit_bytes=mib << 20)


def upward(src, basis, up_leaf, up_mid, pack, half1, coef2, half2, coef):
    leaves, rank, leaf = basis.shape
    mids = up_leaf.shape[0]
    edge = CHILD * leaf
    edge_c = CHILD * rank
    odd = lax.rem(lax.axis_index("leaf"), 2)
    for i in range(leaves):
        coef[pl.ds(i * rank, rank), :] = mm(basis[i], src[pl.ds(i * leaf, leaf), :]).astype(BF16)
    total = None
    for q in range(mids):
        mid = mm(up_leaf[q], coef[pl.ds(q * CHILD * rank, CHILD * rank), :]).astype(BF16)
        pack[pl.ds(q * rank, rank), :] = mid
        lift = mm(up_mid[q], mid).astype(BF16).astype(F32)
        total = lift if total is None else total + lift
    pack[pl.ds(mids * rank, rank), :] = total.astype(BF16)
    far_end = src.shape[0] - edge
    far_end_c = leaves * rank - edge_c
    first = pl.multiple_of((1 - odd) * far_end, leaf)
    second = pl.multiple_of(odd * far_end, leaf)
    first_c = pl.multiple_of((1 - odd) * far_end_c, rank)
    second_c = pl.multiple_of(odd * far_end_c, rank)
    half1[...] = src[pl.ds(first, edge), :]
    half2[...] = src[pl.ds(second, edge), :]
    pack[pl.ds((mids + 1) * rank, edge_c), :] = coef[pl.ds(first_c, edge_c), :]
    coef2[...] = coef[pl.ds(second_c, edge_c), :]


def near_local(index, count, tiles, other, src, out):
    i = pl.program_id(0)
    leaves = pl.num_programs(0)
    slots = tiles.shape[1]
    leaf = tiles.shape[2]
    first = lax.axis_index("leaf") * leaves
    core = lax.axis_index("col")
    live = count[i]
    out[...] = jnp.zeros_like(out)
    for held, mine in ((tiles, core), (other, 1 - core)):
        for k in range(slots):
            slot = mine * slots + k
            at = index[i, slot] - first

            @pl.when((slot < live) & (at >= 0) & (at < leaves))
            def _():
                rows = src[pl.ds(pl.multiple_of(at * leaf, leaf), leaf), :]
                out[...] += mm(held[0, k], rows)


def halo_products(index, count, tiles, other, halo, acc, work, ring, sems, right, leaves, base, acc_base):
    first = lax.axis_index("leaf") * leaves
    core = lax.axis_index("col")
    slots = tiles.shape[1]
    total_slots = 2 * slots
    leaf = tiles.shape[2]

    def note(n, found):
        i = base + n // total_slots
        slot = lax.rem(n, total_slots)
        at = index[i, slot] - first
        outside = jnp.where(right == 1, at - leaves, at + CHILD)
        use = (slot < count[i]) & (outside >= 0) & (outside < CHILD)
        work[0, found] = i
        work[1, found] = slot
        work[2, found] = outside
        return found + use.astype(jnp.int32)

    found = lax.fori_loop(0, CHILD * total_slots, note, jnp.int32(0))

    def fetch(t):
        place = lax.rem(t, RING)
        i = work[0, t]
        slot = work[1, t]
        owner = slot // slots
        k = lax.rem(slot, slots)

        @pl.when(owner == core)
        def _():
            pltpu.make_async_copy(tiles.at[i, k], ring.at[place], sems.at[place]).start()

        @pl.when(owner != core)
        def _():
            pltpu.make_async_copy(other.at[i, k], ring.at[place], sems.at[place]).start()

    lax.fori_loop(0, jnp.minimum(found, RING), lambda t, _: (fetch(t), 0)[1], 0)

    def step(t, _):
        place = lax.rem(t, RING)
        pltpu.make_async_copy(tiles.at[0, 0], ring.at[place], sems.at[place]).wait()
        rows = pl.ds(pl.multiple_of((work[0, t] - acc_base) * leaf, leaf), leaf)
        block = halo[pl.ds(pl.multiple_of(work[2, t] * leaf, leaf), leaf), :]
        acc[rows, :] += mm(ring[place], block)

        @pl.when(t + RING < found)
        def _():
            fetch(t + RING)

        return 0

    lax.fori_loop(0, found, step, 0)


def downward(
    index, count, leaf_far, mid_far,
    acc_in, tiles, other, half1, coef, pack1, coef2, plane, before, after, tops,
    basis, leaf_coupling, up_leaf, mid_coupling, up_mid, top_coupling,
    acc, window, chosen, stack, work, ring, sems,
):
    leaves, rank, leaf = basis.shape
    mids = up_leaf.shape[0]
    group = CHILD // mids
    total_top = top_coupling.shape[0]
    device = lax.axis_index("leaf")
    odd = lax.rem(device, 2)
    parent = device // group
    member = lax.rem(device, group)
    edge_c = CHILD * rank
    top_row = CHILD * rank

    def put_top(value, ahead):
        at = lax.rem(parent + ahead, total_top)
        stack[pl.ds(pl.multiple_of(at * rank, rank), rank), :] = value

    put_top(jnp.zeros((rank, acc.shape[1]), BF16), 0)
    put_top(before[pl.ds(top_row, rank), :], total_top - 1)
    put_top(after[pl.ds(top_row, rank), :], 1)
    for k in range(total_top - 3):
        put_top(tops[pl.ds(k * rank, rank), :], 2 + k)
    top_field = mm(top_coupling[parent], stack[...]).astype(BF16)

    window[pl.ds(edge_c, leaves * rank), :] = coef[...]
    right_at = edge_c + leaves * rank
    at1 = pl.multiple_of((1 - odd) * right_at, rank)
    at2 = pl.multiple_of(odd * right_at, rank)
    window[pl.ds(at1, edge_c), :] = pack1[pl.ds((mids + 1) * rank, edge_c), :]
    window[pl.ds(at2, edge_c), :] = coef2[...]

    for q in range(mids):
        for f in range(FAR):
            b = mid_far[q, f]
            top = b // CHILD
            inside = lax.rem(b, CHILD)
            place = jnp.bitwise_xor(inside // mids, member) * mids + lax.rem(inside, mids)
            row = pl.ds(pl.multiple_of(place * rank, rank), rank)
            to = pl.ds(f * rank, rank)

            @pl.when(top == parent)
            def _():
                chosen[to, :] = plane[row, :]

            @pl.when(top < parent)
            def _():
                chosen[to, :] = before[row, :]

            @pl.when(top > parent)
            def _():
                chosen[to, :] = after[row, :]

        mid_field = (mm(mid_coupling[q], chosen[...]) + mm_t(up_mid[q], top_field)).astype(BF16)
        down = mm_t(up_leaf[q], mid_field)
        for k in range(CHILD):
            i = q * CHILD + k
            for f in range(FAR):
                at = leaf_far[i, f] - (device * leaves - CHILD)
                row = pl.ds(pl.multiple_of(at * rank, rank), rank)
                chosen[pl.ds(f * rank, rank), :] = window[row, :]
            field = (mm(leaf_coupling[i], chosen[...]) + down[k * rank : (k + 1) * rank, :]).astype(BF16)
            rows = pl.ds(i * leaf, leaf)
            acc[rows, :] = acc_in[rows, :] + mm_t(basis[i], field)

    halo_products(
        index, count, tiles, other, half1, acc, work, ring, sems,
        1 - odd, leaves, (1 - odd) * (leaves - CHILD), 0,
    )


def near_last(index, count, acc_in, tiles, other, half2, acc_out, acc, work, ring, sems, acc_sem):
    leaves = tiles.shape[0]
    leaf = tiles.shape[2]
    odd = lax.rem(lax.axis_index("leaf"), 2)
    base = odd * (leaves - CHILD)
    rows = pl.ds(pl.multiple_of(base * leaf, leaf), CHILD * leaf)
    load = pltpu.make_async_copy(acc_in.at[rows], acc, acc_sem)
    load.start()
    load.wait()
    halo_products(index, count, tiles, other, half2, acc, work, ring, sems, odd, leaves, base, base)
    store = pltpu.make_async_copy(acc, acc_out.at[rows], acc_sem)
    store.start()
    store.wait()


def shards(
    sources,
    near_tiles,
    near_index,
    near_count,
    leaf_basis,
    leaf_coupling,
    leaf_far,
    up_leaf,
    mid_coupling,
    mid_far,
    up_mid,
    top_coupling,
):
    sds = jax.ShapeDtypeStruct
    leaves, rank, leaf = leaf_basis.shape
    mids = up_leaf.shape[0]
    cols = sources.shape[1]
    slots = near_tiles.shape[1]
    total_top = top_coupling.shape[0]
    devices = lax.axis_size("leaf")
    group = CHILD // mids
    edge = CHILD * leaf
    edge_c = CHILD * rank
    rows = leaves * leaf

    pair = [(i, i ^ 1) for i in range(devices)]
    rest = [(i, i + 1) for i in range(1, devices - 1, 2)]
    rest = rest + [(j, i) for i, j in rest]

    def shift(k):
        return [(i, (i + k * group) % devices) for i in range(devices)]

    other = lax.ppermute(near_tiles, "col", [(0, 1), (1, 0)])

    pack, half1, coef2, half2, coef = pl.pallas_call(
        upward,
        name="upward",
        out_shape=(
            sds(((mids + 1) * rank + edge_c, cols), BF16),
            sds((edge, cols), BF16),
            sds((edge_c, cols), BF16),
            sds((edge, cols), BF16),
            sds((leaves * rank, cols), BF16),
        ),
        in_specs=[VMEM] * 4,
        out_specs=(VMEM,) * 5,
        compiler_params=params(16),
        cost_estimate=cost(2 * leaves * rank * leaf * cols, 4 << 20),
    )(sources, leaf_basis, up_leaf, up_mid)

    pack1 = lax.ppermute(pack, "leaf", pair)
    half1 = lax.ppermute(half1, "leaf", pair)

    held = mids * rank
    plane = jnp.concatenate([pack[:held], pack1[:held]], axis=0)
    total = pack[held : held + rank].astype(F32) + pack1[held : held + rank].astype(F32)
    total = total.astype(BF16)
    k = 2
    while k < group:
        mine = jnp.concatenate([plane, total], axis=0)
        got = lax.ppermute(mine, "leaf", [(i, i ^ k) for i in range(devices)])
        held = plane.shape[0]
        plane = jnp.concatenate([plane, got[:held]], axis=0)
        total = (total.astype(F32) + got[held:].astype(F32)).astype(BF16)
        k *= 2
    plane = jnp.concatenate([plane, total], axis=0)
    before = lax.ppermute(plane, "leaf", shift(1))
    after = lax.ppermute(plane, "leaf", shift(-1))
    tops = [lax.ppermute(total, "leaf", shift(-k)) for k in range(2, total_top - 1)]
    tops = tops[0] if len(tops) == 1 else jnp.concatenate(tops, axis=0)

    coef2 = lax.ppermute(coef2, "leaf", rest)
    half2 = lax.ppermute(half2, "leaf", rest)

    acc = pl.pallas_call(
        near_local,
        name="near_local",
        out_shape=sds((rows, cols), F32),
        grid_spec=pltpu.PrefetchScalarGridSpec(
            num_scalar_prefetch=2,
            grid=(leaves,),
            in_specs=[
                pl.BlockSpec((1, slots, leaf, leaf), lambda i, *_: (i, 0, 0, 0)),
                pl.BlockSpec((1, slots, leaf, leaf), lambda i, *_: (i, 0, 0, 0)),
                pl.BlockSpec((rows, cols), lambda i, *_: (0, 0)),
            ],
            out_specs=pl.BlockSpec((leaf, cols), lambda i, *_: (i, 0)),
        ),
        compiler_params=params(16),
        cost_estimate=cost(2 * leaves * 2 * slots * leaf * leaf * cols, 24 << 20),
    )(near_index, near_count, near_tiles, other, sources)

    scratch = [
        pltpu.SMEM((3, CHILD * 2 * slots + 1), jnp.int32),
        pltpu.VMEM((RING, leaf, leaf), BF16),
        pltpu.SemaphoreType.DMA((RING,)),
    ]
    acc = pl.pallas_call(
        downward,
        name="downward",
        out_shape=sds((rows, cols), F32),
        in_specs=[SMEM] * 4 + [VMEM, ANY, ANY] + [VMEM] * 14,
        out_specs=VMEM,
        scratch_shapes=[
            pltpu.VMEM((2 * edge_c + leaves * rank, cols), BF16),
            pltpu.VMEM((FAR * rank, cols), BF16),
            pltpu.VMEM((total_top * rank, cols), BF16),
        ]
        + scratch,
        compiler_params=params(32),
        cost_estimate=cost(2 * leaves * slots * leaf * leaf * cols, 12 << 20),
    )(
        near_index, near_count, leaf_far, mid_far,
        acc, near_tiles, other, half1, coef, pack1, coef2, plane, before, after, tops,
        leaf_basis, leaf_coupling, up_leaf, mid_coupling, up_mid, top_coupling,
    )

    return pl.pallas_call(
        near_last,
        name="near_last",
        out_shape=sds((rows, cols), F32),
        in_specs=[SMEM, SMEM, ANY, ANY, ANY, VMEM],
        out_specs=ANY,
        scratch_shapes=[pltpu.VMEM((edge, cols), F32)] + scratch + [pltpu.SemaphoreType.DMA],
        input_output_aliases={2: 0},
        compiler_params=params(16),
        cost_estimate=cost(leaves * slots * leaf * leaf * cols, 4 << 20),
    )(near_index, near_count, acc, near_tiles, other, half2)


def solution(mesh):
    return jax.shard_map(
        shards,
        mesh=mesh,
        in_specs=(
            P("leaf", "col"),
            P("leaf", "col", None, None),
            P("leaf", None),
            P("leaf"),
            P("leaf", None, None),
            P("leaf", None, None),
            P("leaf", None),
            P("leaf", None, None),
            P("leaf", None, None),
            P("leaf", None),
            P("leaf", None, None),
            P(),
        ),
        out_specs=P("leaf", "col"),
        check_vma=False,
    )
```

```python
import jax
import jax.numpy as jnp
from jax import lax
from jax.experimental import pallas as pl
from jax.experimental.pallas import tpu as pltpu
from jax.sharding import PartitionSpec as P


CHILD = 8
FAR = 4
BATCH = 4

F32 = jnp.float32
BF16 = jnp.bfloat16
VMEM = pl.BlockSpec(memory_space=pltpu.VMEM)
SMEM = pl.BlockSpec(memory_space=pltpu.SMEM)
HBM = pl.BlockSpec(memory_space=pltpu.HBM)
ANY = pl.BlockSpec(memory_space=pl.ANY)


def mm(a, b):
    return jnp.dot(a, b, preferred_element_type=F32)


def mm_t(a, b):
    return lax.dot_general(a, b, (((0,), (0,)), ((), ())), preferred_element_type=F32)


def cost(flops, nbytes):
    return pl.CostEstimate(flops=flops, transcendentals=0, bytes_accessed=nbytes)


def params(mib):
    return pltpu.CompilerParams(vmem_limit_bytes=mib << 20)


def in_vmem(x):
    return pltpu.with_memory_space_constraint(x, pltpu.VMEM)


def in_hbm(x):
    return pltpu.with_memory_space_constraint(x, pltpu.HBM)


def blocks(start, count, size):
    return pl.ds(pl.multiple_of(start * size, size), count * size)


def upward(
    src_hbm, basis_hbm, up_leaf_hbm, up_mid_hbm,
    pack, half1, coef2, half2, coef,
    src, basis, up_leaf, up_mid, sems,
):
    loads = [
        pltpu.make_async_copy(a, b, sems.at[k])
        for k, (a, b) in enumerate(
            ((src_hbm, src), (basis_hbm, basis), (up_leaf_hbm, up_leaf), (up_mid_hbm, up_mid))
        )
    ]
    for load in loads:
        load.start()
    leaves, rank, leaf = basis.shape
    mids = up_leaf.shape[0]
    odd = lax.rem(lax.axis_index("leaf"), 2)
    for load in loads:
        load.wait()
    for i in range(leaves):
        coef[pl.ds(i * rank, rank), :] = mm(basis[i], src[pl.ds(i * leaf, leaf), :]).astype(BF16)
    total = None
    for q in range(mids):
        mid = mm(up_leaf[q], coef[pl.ds(q * CHILD * rank, CHILD * rank), :]).astype(BF16)
        pack[pl.ds(q * rank, rank), :] = mid
        lift = mm(up_mid[q], mid).astype(BF16).astype(F32)
        total = lift if total is None else total + lift
    pack[pl.ds(mids * rank, rank), :] = total.astype(BF16)
    first = (1 - odd) * (leaves - CHILD)
    second = odd * (leaves - CHILD)
    half1[...] = src[blocks(first, CHILD, leaf), :]
    half2[...] = src[blocks(second, CHILD, leaf), :]
    pack[pl.ds((mids + 1) * rank, CHILD * rank), :] = coef[blocks(first, CHILD, rank), :]
    coef2[...] = coef[blocks(second, CHILD, rank), :]


def prepare(index, count, tiles_hbm, tiles, work, sem):
    load = pltpu.make_async_copy(tiles_hbm, tiles, sem)
    load.start()
    leaves, slots = tiles.shape[:2]
    room = work.shape[1]
    device = lax.axis_index("leaf")
    odd = lax.rem(device, 2)
    core = lax.axis_index("col")
    first = device * leaves
    base = odd * (leaves - CHILD)

    def clear(n, _):
        for r in range(2):
            work[3 * r, n] = 0
            work[3 * r + 1, n] = 0
            work[3 * r + 2, n] = CHILD
        return 0

    lax.fori_loop(0, room, clear, 0)

    for r, owner in ((0, core), (1, 1 - core)):

        def note(n, found):
            row = n // slots
            k = lax.rem(n, slots)
            slot = owner * slots + k
            at = index[slot, base + row] - first
            outside = jnp.where(odd == 1, at - leaves, at + CHILD)
            use = (slot < count[base + row]) & (outside >= 0) & (outside < CHILD)

            @pl.when(use)
            def _():
                work[3 * r, found] = (base + row) * slots + k
                work[3 * r + 1, found] = outside
                work[3 * r + 2, found] = row

            return found + use.astype(jnp.int32)

        work[6, r] = lax.fori_loop(0, CHILD * slots, note, jnp.int32(0))
    load.wait()


def near_part(index, count, tiles, other, window, out, base, lowest, highest, zero):
    slots, leaf = tiles.shape[1:3]
    leaves = tiles.shape[0]
    first = lax.axis_index("leaf") * leaves
    core = lax.axis_index("col")

    def body(n, _):
        i = base + n
        live = count[i]
        acc = None
        for held, mine in ((tiles, core), (other, 1 - core)):
            for k in range(slots):
                slot = mine * slots + k
                at = index[slot, i] - first
                use = (slot < live) & (at >= lowest) & (at < highest)
                place = jnp.where(use, at - lowest, zero)
                part = mm(held[i, k], window[blocks(place, 1, leaf), :])
                acc = part if acc is None else acc + part
        out[blocks(n, 1, leaf), :] = acc
        return 0

    lax.fori_loop(0, CHILD, body, 0, unroll=2)


def near_own(index, count, tiles, other, src, out, window):
    leaves, _, leaf, _ = tiles.shape
    odd = lax.rem(lax.axis_index("leaf"), 2)
    window[pl.ds(0, leaves * leaf), :] = src[...]
    window[pl.ds(leaves * leaf, leaf), :] = jnp.zeros((leaf, src.shape[1]), BF16)
    near_part(index, count, tiles, other, window, out, odd * (leaves - CHILD), 0, leaves, leaves)


def near_first(index, count, tiles, other, src, half1, out, window):
    leaves, _, leaf, _ = tiles.shape
    odd = lax.rem(lax.axis_index("leaf"), 2)
    total = leaves + CHILD
    window[blocks(odd * CHILD, leaves, leaf), :] = src[...]
    window[blocks((1 - odd) * leaves, CHILD, leaf), :] = half1[...]
    window[pl.ds(total * leaf, leaf), :] = jnp.zeros((leaf, src.shape[1]), BF16)
    lowest = -odd * CHILD
    near_part(
        index, count, tiles, other, window, out,
        (1 - odd) * (leaves - CHILD), lowest, lowest + total, total,
    )


def downward(
    leaf_far, mid_far,
    near1, near2, coef, pack1, coef2, plane, before, after, tops,
    basis, leaf_coupling, up_leaf, mid_coupling, up_mid, top_coupling,
    out, acc2,
    full, window, chosen, stack, sem,
):
    leaves, rank, leaf = basis.shape
    mids = up_leaf.shape[0]
    group = CHILD // mids
    total_top = top_coupling.shape[0]
    device = lax.axis_index("leaf")
    odd = lax.rem(device, 2)
    parent = device // group
    member = lax.rem(device, group)
    top_row = CHILD * rank

    def put_top(value, ahead):
        at = lax.rem(parent + ahead, total_top)
        stack[blocks(at, 1, rank), :] = value

    put_top(jnp.zeros((rank, full.shape[1]), BF16), 0)
    put_top(before[pl.ds(top_row, rank), :], total_top - 1)
    put_top(after[pl.ds(top_row, rank), :], 1)
    for k in range(total_top - 3):
        put_top(tops[pl.ds(k * rank, rank), :], 2 + k)
    top_field = mm(top_coupling[parent], stack[...]).astype(BF16)

    window[pl.ds(CHILD * rank, leaves * rank), :] = coef[...]
    right = CHILD + leaves
    window[blocks((1 - odd) * right, CHILD, rank), :] = pack1[pl.ds((mids + 1) * rank, CHILD * rank), :]
    window[blocks(odd * right, CHILD, rank), :] = coef2[...]

    for q in range(mids):
        for f in range(FAR):
            b = mid_far[q, f]
            top = b // CHILD
            inside = lax.rem(b, CHILD)
            place = jnp.bitwise_xor(inside // mids, member) * mids + lax.rem(inside, mids)
            row = blocks(place, 1, rank)
            to = pl.ds(f * rank, rank)

            @pl.when(top == parent)
            def _():
                chosen[to, :] = plane[row, :]

            @pl.when(top < parent)
            def _():
                chosen[to, :] = before[row, :]

            @pl.when(top > parent)
            def _():
                chosen[to, :] = after[row, :]

        mid_field = (mm(mid_coupling[q], chosen[...]) + mm_t(up_mid[q], top_field)).astype(BF16)
        down = mm_t(up_leaf[q], mid_field)
        for k in range(CHILD):
            i = q * CHILD + k
            picked = [
                window[blocks(leaf_far[f, i] - (device * leaves - CHILD), 1, rank), :]
                for f in range(FAR)
            ]
            field = mm(leaf_coupling[i], jnp.concatenate(picked, axis=0)) + down[k * rank : (k + 1) * rank, :]
            full[pl.ds(i * leaf, leaf), :] = mm_t(basis[i], field.astype(BF16))

    rows1 = blocks((1 - odd) * (leaves - CHILD), CHILD, leaf)
    rows2 = blocks(odd * (leaves - CHILD), CHILD, leaf)
    full[rows1, :] += near1[...]
    store = pltpu.make_async_copy(full.at[rows1], out.at[rows1], sem)
    store.start()
    acc2[...] = full[rows2, :] + near2[...]
    store.wait()


def near_last(work, tiles, other, half2, acc2, out_in, out, acc, sem):
    leaves, slots, leaf, _ = tiles.shape
    odd = lax.rem(lax.axis_index("leaf"), 2)
    acc[pl.ds(0, CHILD * leaf), :] = acc2[...]

    def step(t, _):
        for b in range(BATCH):
            for r, held in ((0, tiles), (1, other)):
                n = t * BATCH + b
                tile = work[3 * r, n]
                part = mm(held[tile // slots, lax.rem(tile, slots)], half2[blocks(work[3 * r + 1, n], 1, leaf), :])
                acc[blocks(work[3 * r + 2, n], 1, leaf), :] += part
        return 0

    longest = jnp.maximum(work[6, 0], work[6, 1])
    lax.fori_loop(0, (longest + BATCH - 1) // BATCH, step, 0)
    rows = blocks(odd * (leaves - CHILD), CHILD, leaf)
    store = pltpu.make_async_copy(acc.at[pl.ds(0, CHILD * leaf)], out.at[rows], sem)
    store.start()
    store.wait()


def shards(
    sources,
    near_tiles,
    near_index,
    near_count,
    leaf_basis,
    leaf_coupling,
    leaf_far,
    up_leaf,
    mid_coupling,
    mid_far,
    up_mid,
    top_coupling,
):
    sds = jax.ShapeDtypeStruct
    leaves, rank, leaf = leaf_basis.shape
    mids = up_leaf.shape[0]
    cols = sources.shape[1]
    slots = near_tiles.shape[1]
    total_top = top_coupling.shape[0]
    devices = lax.axis_size("leaf")
    group = CHILD // mids
    edge = CHILD * leaf
    edge_c = CHILD * rank
    rows = leaves * leaf
    assert leaves == 2 * CHILD and group >= 2 and total_top >= 4
    product_flops = 2 * leaf * leaf * cols

    pair = [(i, i ^ 1) for i in range(devices)]
    rest = [(i, i + 1) for i in range(1, devices - 1, 2)]
    rest = rest + [(j, i) for i, j in rest]

    def shift(k):
        return [(i, (i + k * group) % devices) for i in range(devices)]

    def send(x, pairs, axis="leaf"):
        return lax.ppermute(x, axis, pairs)

    def call(kernel, out_shape, in_specs, out_specs, scratch, mib, estimate, **more):
        def run(*args):
            return pl.pallas_call(
                kernel,
                out_shape=out_shape,
                in_specs=in_specs,
                out_specs=out_specs,
                scratch_shapes=scratch,
                compiler_params=params(mib),
                cost_estimate=estimate,
                **more,
            )(*args)

        return run

    other = in_vmem(send(near_tiles, [(0, 1), (1, 0)], "col"))

    pack, half1, coef2, half2, coef = call(
        upward,
        (
            sds(((mids + 1) * rank + edge_c, cols), BF16),
            sds((edge, cols), BF16),
            sds((edge_c, cols), BF16),
            sds((edge, cols), BF16),
            sds((leaves * rank, cols), BF16),
        ),
        [HBM] * 4,
        (VMEM,) * 5,
        [
            pltpu.VMEM(sources.shape, BF16),
            pltpu.VMEM(leaf_basis.shape, BF16),
            pltpu.VMEM(up_leaf.shape, BF16),
            pltpu.VMEM(up_mid.shape, BF16),
            pltpu.SemaphoreType.DMA((4,)),
        ],
        8,
        cost(2 * leaves * rank * leaf * cols, 4 << 20),
    )(*map(in_hbm, (sources, leaf_basis, up_leaf, up_mid)))

    pack1 = send(pack, pair)
    half1 = send(half1, pair)

    index = near_index.T
    most = CHILD * slots
    tiles, work = call(
        prepare,
        (sds(near_tiles.shape, BF16), sds((7, most + BATCH), jnp.int32)),
        [SMEM, SMEM, HBM],
        (VMEM, SMEM),
        [pltpu.SemaphoreType.DMA],
        12,
        cost(0, near_tiles.size * 2),
    )(index, near_count, in_hbm(near_tiles))
    tiles = in_vmem(tiles)

    held = mids * rank
    plane = jnp.concatenate([pack[:held], pack1[:held]], axis=0)
    total = pack[held : held + rank].astype(F32) + pack1[held : held + rank].astype(F32)
    total = total.astype(BF16)
    k = 2
    while k < group:
        mine = jnp.concatenate([plane, total], axis=0)
        got = send(mine, [(i, i ^ k) for i in range(devices)])
        held = plane.shape[0]
        plane = jnp.concatenate([plane, got[:held]], axis=0)
        total = (total.astype(F32) + got[held:].astype(F32)).astype(BF16)
        k *= 2
    plane = jnp.concatenate([plane, total], axis=0)
    before = send(plane, shift(1))
    after = send(plane, shift(-1))
    tops = [send(total, shift(-k)) for k in range(2, total_top - 1)]
    tops = tops[0] if len(tops) == 1 else jnp.concatenate(tops, axis=0)

    coef2 = send(coef2, rest)
    half2 = send(half2, rest)

    near2 = call(
        near_own,
        sds((edge, cols), F32),
        [SMEM, SMEM, VMEM, VMEM, VMEM],
        VMEM,
        [pltpu.VMEM((rows + leaf, cols), BF16)],
        8,
        cost(CHILD * 2 * slots * product_flops, 16 << 20),
    )(index, near_count, tiles, other, sources)

    near1 = call(
        near_first,
        sds((edge, cols), F32),
        [SMEM, SMEM, VMEM, VMEM, VMEM, VMEM],
        VMEM,
        [pltpu.VMEM((rows + edge + leaf, cols), BF16)],
        8,
        cost(CHILD * 2 * slots * product_flops, 16 << 20),
    )(index, near_count, tiles, other, sources, half1)

    out, acc2 = call(
        downward,
        (sds((rows, cols), F32), sds((edge, cols), F32)),
        [SMEM] * 2 + [VMEM] * 15,
        (ANY, VMEM),
        [
            pltpu.VMEM((rows, cols), F32),
            pltpu.VMEM((2 * edge_c + leaves * rank, cols), BF16),
            pltpu.VMEM((FAR * rank, cols), BF16),
            pltpu.VMEM((total_top * rank, cols), BF16),
            pltpu.SemaphoreType.DMA,
        ],
        20,
        cost(leaves * 4 * product_flops, 12 << 20),
    )(
        leaf_far.T, mid_far,
        near1, near2, coef, pack1, coef2, plane, before, after, tops,
        leaf_basis, leaf_coupling, up_leaf, mid_coupling, up_mid, top_coupling,
    )

    return call(
        near_last,
        sds((rows, cols), F32),
        [SMEM, VMEM, VMEM, VMEM, VMEM, ANY],
        ANY,
        [pltpu.VMEM((edge + leaf, cols), F32), pltpu.SemaphoreType.DMA],
        8,
        cost(leaves * slots * product_flops, 4 << 20),
        input_output_aliases={5: 0},
    )(work, tiles, other, half2, acc2, out)


def solution(mesh):


    return jax.shard_map(
        shards,
        mesh=mesh,
        in_specs=(
            P("leaf", "col"),
            P("leaf", "col", None, None),
            P("leaf", None),
            P("leaf"),
            P("leaf", None, None),
            P("leaf", None, None),
            P("leaf", None),
            P("leaf", None, None),
            P("leaf", None, None),
            P("leaf", None),
            P("leaf", None, None),
            P(),
        ),
        out_specs=P("leaf", "col"),
        check_vma=False,
    )
```

```python
import jax
import jax.numpy as jnp
from jax import lax
from jax.experimental import pallas as pl
from jax.experimental.pallas import tpu as pltpu
from jax.sharding import PartitionSpec as P


CHILD = 8
FAR = 4
BATCH = 4
PARTS = 4

F32 = jnp.float32
BF16 = jnp.bfloat16
VMEM = pl.BlockSpec(memory_space=pltpu.VMEM)
SMEM = pl.BlockSpec(memory_space=pltpu.SMEM)
HBM = pl.BlockSpec(memory_space=pltpu.HBM)
ANY = pl.BlockSpec(memory_space=pl.ANY)


def mm(a, b):
    return jnp.dot(a, b, preferred_element_type=F32)


def mm_t(a, b):
    return lax.dot_general(a, b, (((0,), (0,)), ((), ())), preferred_element_type=F32)


def cost(flops, nbytes):
    return pl.CostEstimate(flops=flops, transcendentals=0, bytes_accessed=nbytes)


def params(mib):
    return pltpu.CompilerParams(vmem_limit_bytes=mib << 20)


def in_vmem(x):
    return pltpu.with_memory_space_constraint(x, pltpu.VMEM)


def in_hbm(x):
    return pltpu.with_memory_space_constraint(x, pltpu.HBM)


def blocks(start, count, size):
    return pl.ds(pl.multiple_of(start * size, size), count * size)


def upward(
    src_hbm, basis_hbm, up_leaf_hbm, up_mid_hbm,
    pack, half1, coef2, half2, coef,
    src, basis, up_leaf, up_mid, sems,
):
    leaves, rank, leaf = basis.shape
    mids = up_leaf.shape[0]
    step = leaves // PARTS
    loads = []
    for p in range(PARTS):
        near = pl.ds(p * step * leaf, step * leaf)
        far = pl.ds(p * step, step)
        loads.append(pltpu.make_async_copy(src_hbm.at[near], src.at[near], sems.at[2 * p]))
        loads.append(pltpu.make_async_copy(basis_hbm.at[far], basis.at[far], sems.at[2 * p + 1]))
    loads.append(pltpu.make_async_copy(up_leaf_hbm, up_leaf, sems.at[2 * PARTS]))
    loads.append(pltpu.make_async_copy(up_mid_hbm, up_mid, sems.at[2 * PARTS + 1]))
    for load in loads:
        load.start()
    odd = lax.rem(lax.axis_index("leaf"), 2)
    for p in range(PARTS):
        loads[2 * p].wait()
        loads[2 * p + 1].wait()
        for i in range(p * step, (p + 1) * step):
            coef[pl.ds(i * rank, rank), :] = mm(basis[i], src[pl.ds(i * leaf, leaf), :]).astype(BF16)
    first = (1 - odd) * (leaves - CHILD)
    second = odd * (leaves - CHILD)
    pack[pl.ds((mids + 1) * rank, CHILD * rank), :] = coef[blocks(first, CHILD, rank), :]
    coef2[...] = coef[blocks(second, CHILD, rank), :]
    half1[...] = src[blocks(first, CHILD, leaf), :]
    half2[...] = src[blocks(second, CHILD, leaf), :]
    loads[2 * PARTS].wait()
    loads[2 * PARTS + 1].wait()
    total = None
    for q in range(mids):
        mid = mm(up_leaf[q], coef[pl.ds(q * CHILD * rank, CHILD * rank), :]).astype(BF16)
        pack[pl.ds(q * rank, rank), :] = mid
        lift = mm(up_mid[q], mid).astype(BF16).astype(F32)
        total = lift if total is None else total + lift
    pack[pl.ds(mids * rank, rank), :] = total.astype(BF16)


def lists(index, count, work):
    leaves = index.shape[1]
    slots = index.shape[0] // 2
    device = lax.axis_index("leaf")
    odd = lax.rem(device, 2)
    core = lax.axis_index("col")
    first = device * leaves
    base = odd * (leaves - CHILD)
    lowest = jnp.where(odd == 1, leaves, -CHILD) + first

    def row(n, found):
        live = count[base + n]
        out = []
        for r, owner in ((0, core), (1, 1 - core)):
            at = found[r]
            for k in range(slots):
                slot = owner * slots + k
                outside = index[slot, base + n] - lowest
                work[3 * r, at] = n * slots + k
                work[3 * r + 1, at] = outside
                work[3 * r + 2, at] = n
                use = (slot < live) & (outside >= 0) & (outside < CHILD)
                at = at + use.astype(jnp.int32)
            out.append(at)
        return tuple(out)

    found = lax.fori_loop(0, CHILD, row, (jnp.int32(0), jnp.int32(0)))
    longest = jnp.maximum(found[0], found[1])
    rounds = (longest + BATCH - 1) // BATCH
    work[6, 0] = rounds
    for r in range(2):

        def fill(n, _):
            work[3 * r, n] = 0
            work[3 * r + 1, n] = 0
            work[3 * r + 2, n] = CHILD
            return 0

        lax.fori_loop(found[r], rounds * BATCH, fill, 0)


def load_tiles(tiles_hbm, tiles, sems, base):
    leaves = tiles.shape[0]
    loads = [
        pltpu.make_async_copy(tiles_hbm.at[base + n], tiles.at[n], sems.at[n]) for n in range(leaves)
    ]
    for load in loads:
        load.start()
    return loads


def place_of(index, live, slot, i, lowest, total):
    at = index[slot, i] - lowest
    return jnp.where((slot < live) & (at >= 0) & (at < total), at, total)


def near_a(index, count, tiles_hbm, src, out, tiles, window, sems, sem):
    slots, leaf = tiles.shape[1:3]
    leaves = tiles_hbm.shape[0]
    own = pltpu.make_async_copy(src, window.at[pl.ds(0, leaves * leaf)], sem)
    own.start()
    device = lax.axis_index("leaf")
    base = lax.rem(device, 2) * (leaves - CHILD)
    loads = load_tiles(tiles_hbm, tiles, sems, base)
    core = lax.axis_index("col")
    window[pl.ds(leaves * leaf, leaf), :] = jnp.zeros((leaf, src.shape[1]), BF16)
    own.wait()
    for n in range(CHILD):
        i = base + n
        live = count[i]
        loads[n].wait()
        acc = None
        for k in range(slots):
            place = place_of(index, live, core * slots + k, i, device * leaves, leaves)
            part = mm(tiles[n, k], window[blocks(place, 1, leaf), :])
            acc = part if acc is None else acc + part
        out[pl.ds(n * leaf, leaf), :] = acc


def near_mid(
    index, count, tiles_hbm, other, src, half1, far, near2,
    out, acc2,
    tiles, window, full, sems, sem,
):
    slots, leaf = tiles.shape[1:3]
    leaves = tiles_hbm.shape[0]
    device = lax.axis_index("leaf")
    odd = lax.rem(device, 2)
    core = lax.axis_index("col")
    base1 = (1 - odd) * (leaves - CHILD)
    base2 = odd * (leaves - CHILD)
    total = leaves + CHILD
    own = pltpu.make_async_copy(src, window.at[blocks(odd * CHILD, leaves, leaf)], sem)
    own.start()
    load_tiles(tiles_hbm, tiles, sems, base1)
    window[blocks((1 - odd) * leaves, CHILD, leaf), :] = half1[...]
    window[pl.ds(total * leaf, leaf), :] = jnp.zeros((leaf, src.shape[1]), BF16)
    lowest = device * leaves - odd * CHILD
    own.wait()

    def product(held, n, k, slot, i, live):
        place = place_of(index, live, slot, i, lowest, total)
        return mm(held[n, k], window[blocks(place, 1, leaf), :])

    def first_half(n, _):
        i = base1 + n
        live = count[i]
        pltpu.make_async_copy(tiles_hbm.at[0], tiles.at[n], sems.at[n]).wait()
        acc = far[blocks(i, 1, leaf), :]
        for k in range(slots):
            acc += product(other, i, k, (1 - core) * slots + k, i, live)
        for k in range(slots):
            acc += product(tiles, n, k, core * slots + k, i, live)
        full[blocks(n, 1, leaf), :] = acc
        return 0

    lax.fori_loop(0, CHILD, first_half, 0, unroll=2)
    store = pltpu.make_async_copy(full, out.at[blocks(base1, CHILD, leaf)], sem)
    store.start()

    def second_half(n, _):
        i = base2 + n
        live = count[i]
        acc = far[blocks(i, 1, leaf), :] + near2[blocks(n, 1, leaf), :]
        for k in range(slots):
            acc += product(other, i, k, (1 - core) * slots + k, i, live)
        acc2[blocks(n, 1, leaf), :] = acc
        return 0

    lax.fori_loop(0, CHILD, second_half, 0, unroll=2)
    store.wait()


def downward(
    leaf_far, mid_far,
    coef, pack1, coef2, plane, before, after, tops,
    basis, leaf_coupling, up_leaf, mid_coupling, up_mid, top_coupling,
    far,
    window, chosen, stack,
):
    leaves, rank, leaf = basis.shape
    mids = up_leaf.shape[0]
    group = CHILD // mids
    total_top = top_coupling.shape[0]
    device = lax.axis_index("leaf")
    odd = lax.rem(device, 2)
    parent = device // group
    member = lax.rem(device, group)
    top_row = CHILD * rank

    def put_top(value, ahead):
        at = lax.rem(parent + ahead, total_top)
        stack[blocks(at, 1, rank), :] = value

    put_top(jnp.zeros((rank, far.shape[1]), BF16), 0)
    put_top(before[pl.ds(top_row, rank), :], total_top - 1)
    put_top(after[pl.ds(top_row, rank), :], 1)
    for k in range(total_top - 3):
        put_top(tops[pl.ds(k * rank, rank), :], 2 + k)
    top_field = mm(top_coupling[parent], stack[...]).astype(BF16)

    window[pl.ds(CHILD * rank, leaves * rank), :] = coef[...]
    right = CHILD + leaves
    window[blocks((1 - odd) * right, CHILD, rank), :] = pack1[pl.ds((mids + 1) * rank, CHILD * rank), :]
    window[blocks(odd * right, CHILD, rank), :] = coef2[...]

    for q in range(mids):
        for f in range(FAR):
            b = mid_far[q, f]
            top = b // CHILD
            inside = lax.rem(b, CHILD)
            place = jnp.bitwise_xor(inside // mids, member) * mids + lax.rem(inside, mids)
            row = blocks(place, 1, rank)
            to = pl.ds(f * rank, rank)

            @pl.when(top == parent)
            def _():
                chosen[to, :] = plane[row, :]

            @pl.when(top < parent)
            def _():
                chosen[to, :] = before[row, :]

            @pl.when(top > parent)
            def _():
                chosen[to, :] = after[row, :]

        mid_field = (mm(mid_coupling[q], chosen[...]) + mm_t(up_mid[q], top_field)).astype(BF16)
        down = mm_t(up_leaf[q], mid_field)
        for k in range(CHILD):
            i = q * CHILD + k
            picked = [
                window[blocks(leaf_far[f, i] - (device * leaves - CHILD), 1, rank), :]
                for f in range(FAR)
            ]
            field = mm(leaf_coupling[i], jnp.concatenate(picked, axis=0)) + down[k * rank : (k + 1) * rank, :]
            far[pl.ds(i * leaf, leaf), :] = mm_t(basis[i], field.astype(BF16))


def near_last(work, tiles, other, half2, acc2, out_in, out, acc, sem):
    leaves, slots, leaf, _ = other.shape
    odd = lax.rem(lax.axis_index("leaf"), 2)
    base = odd * (leaves - CHILD)
    acc[pl.ds(0, CHILD * leaf), :] = acc2[...]

    def step(t, _):
        for b in range(BATCH):
            n = t * BATCH + b
            for r, held, low in ((0, tiles, 0), (1, other, base)):
                tile = work[3 * r, n]
                part = mm(
                    held[low + tile // slots, lax.rem(tile, slots)],
                    half2[blocks(work[3 * r + 1, n], 1, leaf), :],
                )
                acc[blocks(work[3 * r + 2, n], 1, leaf), :] += part
        return 0

    lax.fori_loop(0, work[6, 0], step, 0)
    rows = blocks(base, CHILD, leaf)
    store = pltpu.make_async_copy(acc.at[pl.ds(0, CHILD * leaf)], out.at[rows], sem)
    store.start()
    store.wait()


def shards(
    sources,
    near_tiles,
    near_index,
    near_count,
    leaf_basis,
    leaf_coupling,
    leaf_far,
    up_leaf,
    mid_coupling,
    mid_far,
    up_mid,
    top_coupling,
):
    sds = jax.ShapeDtypeStruct
    leaves, rank, leaf = leaf_basis.shape
    mids = up_leaf.shape[0]
    cols = sources.shape[1]
    slots = near_tiles.shape[1]
    total_top = top_coupling.shape[0]
    devices = lax.axis_size("leaf")
    group = CHILD // mids
    edge = CHILD * leaf
    edge_c = CHILD * rank
    rows = leaves * leaf
    assert leaves == 2 * CHILD and group >= 2 and total_top >= 4
    product_flops = 2 * leaf * leaf * cols

    pair = [(i, i ^ 1) for i in range(devices)]
    rest = [(i, i + 1) for i in range(1, devices - 1, 2)]
    rest = rest + [(j, i) for i, j in rest]

    def shift(k):
        return [(i, (i + k * group) % devices) for i in range(devices)]

    def send(x, pairs, axis="leaf"):
        return lax.ppermute(x, axis, pairs)

    def call(kernel, out_shape, in_specs, out_specs, scratch, mib, estimate, **more):
        def run(*args):
            return pl.pallas_call(
                kernel,
                out_shape=out_shape,
                in_specs=in_specs,
                out_specs=out_specs,
                scratch_shapes=scratch,
                compiler_params=params(mib),
                cost_estimate=estimate,
                **more,
            )(*args)

        return run

    index, count, far_index, mid_index = map(in_hbm, (near_index.T, near_count, leaf_far.T, mid_far))
    own_tiles = in_hbm(near_tiles)

    pack, half1, coef2, half2, coef = call(
        upward,
        (
            sds(((mids + 1) * rank + edge_c, cols), BF16),
            sds((edge, cols), BF16),
            sds((edge_c, cols), BF16),
            sds((edge, cols), BF16),
            sds((leaves * rank, cols), BF16),
        ),
        [HBM] * 4,
        (VMEM,) * 5,
        [
            pltpu.VMEM(sources.shape, BF16),
            pltpu.VMEM(leaf_basis.shape, BF16),
            pltpu.VMEM(up_leaf.shape, BF16),
            pltpu.VMEM(up_mid.shape, BF16),
            pltpu.SemaphoreType.DMA((2 * PARTS + 2,)),
        ],
        8,
        cost(2 * leaves * rank * leaf * cols, 4 << 20),
    )(*map(in_hbm, (sources, leaf_basis, up_leaf, up_mid)))

    pack1 = send(pack, pair)
    coef2 = send(coef2, rest)
    half1 = send(half1, pair)
    other = in_vmem(send(near_tiles, [(0, 1), (1, 0)], "col"))

    work = call(
        lists,
        sds((7, CHILD * slots + BATCH), jnp.int32),
        [SMEM, SMEM],
        SMEM,
        [],
        8,
        cost(0, 1 << 20),
    )(index, count)

    held = mids * rank
    plane = jnp.concatenate([pack[:held], pack1[:held]], axis=0)
    total = pack[held : held + rank].astype(F32) + pack1[held : held + rank].astype(F32)
    total = total.astype(BF16)
    k = 2
    while k < group:
        mine = jnp.concatenate([plane, total], axis=0)
        got = send(mine, [(i, i ^ k) for i in range(devices)])
        held = plane.shape[0]
        plane = jnp.concatenate([plane, got[:held]], axis=0)
        total = (total.astype(F32) + got[held:].astype(F32)).astype(BF16)
        k *= 2
    half2 = send(half2, rest)

    near2, tiles2 = call(
        near_a,
        (sds((edge, cols), F32), sds((CHILD,) + near_tiles.shape[1:], BF16)),
        [SMEM, SMEM, HBM, HBM],
        (VMEM, VMEM),
        [
            pltpu.VMEM((rows + leaf, cols), BF16),
            pltpu.SemaphoreType.DMA((CHILD,)),
            pltpu.SemaphoreType.DMA,
        ],
        12,
        cost(CHILD * slots * product_flops, 8 << 20),
    )(index, count, own_tiles, in_hbm(sources))
    tiles2 = in_vmem(tiles2)

    plane = jnp.concatenate([plane, total], axis=0)
    before = send(plane, shift(1))
    after = send(plane, shift(-1))
    tops = [send(total, shift(-k)) for k in range(2, total_top - 1)]
    tops = tops[0] if len(tops) == 1 else jnp.concatenate(tops, axis=0)

    far = call(
        downward,
        sds((rows, cols), F32),
        [SMEM] * 2 + [VMEM] * 13,
        VMEM,
        [
            pltpu.VMEM((2 * edge_c + leaves * rank, cols), BF16),
            pltpu.VMEM((FAR * rank, cols), BF16),
            pltpu.VMEM((total_top * rank, cols), BF16),
        ],
        16,
        cost(leaves * 4 * product_flops, 12 << 20),
    )(
        far_index, mid_index,
        coef, pack1, coef2, plane, before, after, tops,
        leaf_basis, leaf_coupling, up_leaf, mid_coupling, up_mid, top_coupling,
    )

    out, acc2 = call(
        near_mid,
        (sds((rows, cols), F32), sds((edge, cols), F32)),
        [SMEM, SMEM, HBM, VMEM, HBM] + [VMEM] * 3,
        (ANY, VMEM),
        [
            pltpu.VMEM((CHILD,) + near_tiles.shape[1:], BF16),
            pltpu.VMEM((rows + edge + leaf, cols), BF16),
            pltpu.VMEM((edge, cols), F32),
            pltpu.SemaphoreType.DMA((CHILD,)),
            pltpu.SemaphoreType.DMA,
        ],
        16,
        cost(CHILD * 3 * slots * product_flops, 16 << 20),
    )(index, count, own_tiles, other, in_hbm(sources), half1, far, near2)

    return call(
        near_last,
        sds((rows, cols), F32),
        [SMEM, VMEM, VMEM, VMEM, VMEM, ANY],
        ANY,
        [pltpu.VMEM((edge + leaf, cols), F32), pltpu.SemaphoreType.DMA],
        8,
        cost(leaves * slots * product_flops, 4 << 20),
        input_output_aliases={5: 0},
    )(work, tiles2, other, half2, acc2, out)


def solution(mesh):


    return jax.shard_map(
        shards,
        mesh=mesh,
        in_specs=(
            P("leaf", "col"),
            P("leaf", "col", None, None),
            P("leaf", None),
            P("leaf"),
            P("leaf", None, None),
            P("leaf", None, None),
            P("leaf", None),
            P("leaf", None, None),
            P("leaf", None, None),
            P("leaf", None),
            P("leaf", None, None),
            P(),
        ),
        out_specs=P("leaf", "col"),
        check_vma=False,
    )
```

```python
import jax
import jax.numpy as jnp
from jax import lax
from jax.experimental import pallas as pl
from jax.experimental.pallas import tpu as pltpu
from jax.sharding import PartitionSpec as P


CHILD = 8
FAR = 4
BATCH = 4
PARTS = 4

F32 = jnp.float32
BF16 = jnp.bfloat16
VMEM = pl.BlockSpec(memory_space=pltpu.VMEM)
SMEM = pl.BlockSpec(memory_space=pltpu.SMEM)
HBM = pl.BlockSpec(memory_space=pltpu.HBM)
ANY = pl.BlockSpec(memory_space=pl.ANY)


def mm(a, b):
    return jnp.dot(a, b, preferred_element_type=F32)


def mm_t(a, b):
    return lax.dot_general(a, b, (((0,), (0,)), ((), ())), preferred_element_type=F32)


def cost(flops, nbytes):
    return pl.CostEstimate(flops=flops, transcendentals=0, bytes_accessed=nbytes)


def params(mib):
    return pltpu.CompilerParams(vmem_limit_bytes=mib << 20)


def in_vmem(x):
    return pltpu.with_memory_space_constraint(x, pltpu.VMEM)


def in_hbm(x):
    return pltpu.with_memory_space_constraint(x, pltpu.HBM)


def blocks(start, count, size):
    return pl.ds(pl.multiple_of(start * size, size), count * size)


def upward(
    src_hbm, basis_hbm, up_leaf_hbm, up_mid_hbm,
    pack, bulk1, coef, src,
    basis, up_leaf, up_mid, sems,
):
    leaves, rank, leaf = basis.shape
    mids = up_leaf.shape[0]
    step = leaves // PARTS
    loads = []
    for p in range(PARTS):
        near = pl.ds(p * step * leaf, step * leaf)
        far = pl.ds(p * step, step)
        loads.append(pltpu.make_async_copy(src_hbm.at[near], src.at[near], sems.at[2 * p]))
        loads.append(pltpu.make_async_copy(basis_hbm.at[far], basis.at[far], sems.at[2 * p + 1]))
    loads.append(pltpu.make_async_copy(up_leaf_hbm, up_leaf, sems.at[2 * PARTS]))
    loads.append(pltpu.make_async_copy(up_mid_hbm, up_mid, sems.at[2 * PARTS + 1]))
    for load in loads:
        load.start()
    src[pl.ds(leaves * leaf, leaf), :] = jnp.zeros((leaf, src.shape[1]), BF16)
    odd = lax.rem(lax.axis_index("leaf"), 2)
    for p in range(PARTS):
        loads[2 * p].wait()
        loads[2 * p + 1].wait()
        for i in range(p * step, (p + 1) * step):
            coef[pl.ds(i * rank, rank), :] = mm(basis[i], src[pl.ds(i * leaf, leaf), :]).astype(BF16)
    first = (1 - odd) * (leaves - CHILD)
    bulk1[pl.ds(0, CHILD * rank), :] = coef[blocks(first, CHILD, rank), :]
    bulk1[pl.ds(CHILD * rank, CHILD * leaf), :] = src[blocks(first, CHILD, leaf), :]
    loads[2 * PARTS].wait()
    loads[2 * PARTS + 1].wait()
    total = None
    for q in range(mids):
        mid = mm(up_leaf[q], coef[pl.ds(q * CHILD * rank, CHILD * rank), :]).astype(BF16)
        pack[pl.ds(q * rank, rank), :] = mid
        lift = mm(up_mid[q], mid).astype(BF16).astype(F32)
        total = lift if total is None else total + lift
    pack[pl.ds(mids * rank, rank), :] = total.astype(BF16)


def prepare(index, count, coef, src, work, bulk2):
    leaves = index.shape[1]
    slots = index.shape[0] // 2
    rank = coef.shape[0] // leaves
    leaf = src.shape[0] // (leaves + 1)
    device = lax.axis_index("leaf")
    odd = lax.rem(device, 2)
    core = lax.axis_index("col")
    base = odd * (leaves - CHILD)
    bulk2[pl.ds(0, CHILD * rank), :] = coef[blocks(base, CHILD, rank), :]
    bulk2[pl.ds(CHILD * rank, CHILD * leaf), :] = src[blocks(base, CHILD, leaf), :]
    lowest = jnp.where(odd == 1, leaves, -CHILD) + device * leaves

    def row(n, found):
        live = count[base + n]
        out = []
        for r, owner in ((0, core), (1, 1 - core)):
            at = found[r]
            for k in range(slots):
                slot = owner * slots + k
                outside = index[slot, base + n] - lowest
                work[3 * r, at] = n * slots + k
                work[3 * r + 1, at] = outside
                work[3 * r + 2, at] = n
                use = (slot < live) & (outside >= 0) & (outside < CHILD)
                at = at + use.astype(jnp.int32)
            out.append(at)
        return tuple(out)

    found = lax.fori_loop(0, CHILD, row, (jnp.int32(0), jnp.int32(0)))
    longest = jnp.maximum(found[0], found[1])
    rounds = (longest + BATCH - 1) // BATCH
    work[6, 0] = rounds
    for r in range(2):

        def fill(n, _):
            work[3 * r, n] = 0
            work[3 * r + 1, n] = 0
            work[3 * r + 2, n] = CHILD
            return 0

        lax.fori_loop(found[r], rounds * BATCH, fill, 0)


def load_tiles(tiles_hbm, tiles, sems, base):
    loads = [
        pltpu.make_async_copy(tiles_hbm.at[base + n], tiles.at[n], sems.at[n])
        for n in range(tiles.shape[0])
    ]
    for load in loads:
        load.start()
    return loads


def product(index, live, held, n, k, slot, i, window, lowest, total):
    leaf = held.shape[3]
    at = index[slot, i] - lowest
    place = jnp.where((slot < live) & (at >= 0) & (at < total), at, total)
    return mm(held[n, k], window[blocks(place, 1, leaf), :])


def near_most(index, count, tiles_hbm, other, src, bulk1, acc1, acc2, tiles2, tiles1, window, sems1, sems2):
    leaves, slots, leaf, _ = other.shape
    device = lax.axis_index("leaf")
    odd = lax.rem(device, 2)
    core = lax.axis_index("col")
    base1 = (1 - odd) * (leaves - CHILD)
    base2 = odd * (leaves - CHILD)
    loads2 = load_tiles(tiles_hbm, tiles2, sems2, base2)
    loads1 = load_tiles(tiles_hbm, tiles1, sems1, base1)
    total = leaves + CHILD
    window[blocks(odd * CHILD, leaves, leaf), :] = src[pl.ds(0, leaves * leaf), :]
    window[blocks((1 - odd) * leaves, CHILD, leaf), :] = bulk1[pl.ds(bulk1.shape[0] - CHILD * leaf, CHILD * leaf), :]
    window[pl.ds(total * leaf, leaf), :] = jnp.zeros((leaf, src.shape[1]), BF16)
    lowest = device * leaves - odd * CHILD

    def others2(n, _):
        i = base2 + n
        acc2[blocks(n, 1, leaf), :] = sum(
            product(index, count[i], other, i, k, (1 - core) * slots + k, i, src, device * leaves, leaves)
            for k in range(slots)
        )
        return 0

    lax.fori_loop(0, CHILD, others2, 0, unroll=4)
    for load in loads2:
        load.wait()

    def own2(n, _):
        i = base2 + n
        acc2[blocks(n, 1, leaf), :] += sum(
            product(index, count[i], tiles2, n, k, core * slots + k, i, src, device * leaves, leaves)
            for k in range(slots)
        )
        return 0

    lax.fori_loop(0, CHILD, own2, 0, unroll=4)
    for load in loads1:
        load.wait()

    def all1(n, _):
        i = base1 + n
        acc1[blocks(n, 1, leaf), :] = sum(
            product(index, count[i], held, at, k, owner * slots + k, i, window, lowest, total)
            for held, at, owner in ((tiles1, n, core), (other, i, 1 - core))
            for k in range(slots)
        )
        return 0

    lax.fori_loop(0, CHILD, all1, 0, unroll=2)


def downward(
    leaf_far, mid_far,
    near1, near2, coef, bulk1, plane, next_a, next_b,
    basis, leaf_coupling, up_leaf, mid_coupling, up_mid, top_coupling,
    *refs,
):
    total_top = top_coupling.shape[0]
    tops = refs[: total_top - 1]
    out, acc2, turned, full, down, window, chosen, stack, sems = refs[total_top - 1 :]
    leaves, rank, leaf = basis.shape
    mids = up_leaf.shape[0]
    group = CHILD // mids
    device = lax.axis_index("leaf")
    odd = lax.rem(device, 2)
    parent = device // group
    member = lax.rem(device, group)

    stack[blocks(parent, 1, rank), :] = jnp.zeros((rank, full.shape[1]), BF16)
    for p in range(1, total_top):
        stack[blocks(jnp.bitwise_xor(parent, p), 1, rank), :] = tops[p - 1][...]
    top_field = mm(top_coupling[parent], stack[...]).astype(BF16)

    total = leaves + CHILD
    lowest = device * leaves - odd * CHILD
    window[blocks(odd * CHILD, leaves, rank), :] = coef[...]
    window[blocks((1 - odd) * leaves, CHILD, rank), :] = bulk1[pl.ds(0, CHILD * rank), :]
    window[pl.ds(total * rank, rank), :] = jnp.zeros((rank, full.shape[1]), BF16)

    for q in range(mids):
        for f in range(FAR):
            b = mid_far[q, f]
            above = b // CHILD
            inside = lax.rem(b, CHILD)
            place = jnp.bitwise_xor(inside // mids, member) * mids + lax.rem(inside, mids)
            row = blocks(place, 1, rank)
            to = pl.ds((q * FAR + f) * rank, rank)
            beside = jnp.bitwise_xor(parent, 1)

            @pl.when(above == parent)
            def _():
                chosen[to, :] = plane[row, :]

            @pl.when(above == beside)
            def _():
                chosen[to, :] = next_a[row, :]

            @pl.when((above != parent) & (above != beside))
            def _():
                chosen[to, :] = next_b[row, :]

    for q in range(mids):
        picked = chosen[pl.ds(q * FAR * rank, FAR * rank), :]
        mid_field = (mm(mid_coupling[q], picked) + mm_t(up_mid[q], top_field)).astype(BF16)
        down[pl.ds(q * CHILD * rank, CHILD * rank), :] = mm_t(up_leaf[q], mid_field)

    def field_of(i):
        field = far_sum(leaf_far, leaf_coupling, window, i, lowest, total)
        return (field + down[blocks(i, 1, rank), :]).astype(BF16)

    base1 = (1 - odd) * (leaves - CHILD)
    base2 = odd * (leaves - CHILD)
    stores = []
    for n in range(CHILD):
        rows = pl.ds(n * leaf, leaf)
        full[rows, :] = near1[rows, :] + mm_t(basis[base1 + n], field_of(base1 + n))
        if n % 2 == 1:
            rows = pl.ds((n - 1) * leaf, 2 * leaf)
            stores.append(
                pltpu.make_async_copy(full.at[rows], out.at[blocks(base1 + n - 1, 2, leaf)], sems.at[n // 2])
            )
            stores[-1].start()
    for n in range(CHILD):
        rows = pl.ds(n * leaf, leaf)
        turned[n] = basis[base2 + n].T
        acc2[rows, :] = near2[rows, :] + mm(turned[n], field_of(base2 + n))
    for store in stores:
        store.wait()


def far_sum(leaf_far, leaf_coupling, window, i, lowest, total):
    rank = leaf_coupling.shape[1]
    picked = []
    for f in range(FAR):
        at = leaf_far[f, i] - lowest
        place = jnp.where((at >= 0) & (at < total), at, total)
        picked.append(window[blocks(place, 1, rank), :])
    return mm(leaf_coupling[i], jnp.concatenate(picked, axis=0))


def near_last(work, leaf_far, tiles, other, bulk2, acc_in, leaf_coupling, turned, out_in, out, acc, window, sems):
    leaves, slots, leaf, _ = other.shape
    rank = leaf_coupling.shape[1]
    device = lax.axis_index("leaf")
    odd = lax.rem(device, 2)
    base = odd * (leaves - CHILD)
    window[pl.ds(0, CHILD * rank), :] = bulk2[pl.ds(0, CHILD * rank), :]
    window[pl.ds(CHILD * rank, rank), :] = jnp.zeros((rank, bulk2.shape[1]), BF16)
    lowest = device * leaves + jnp.where(odd == 1, leaves, -CHILD)
    for n in range(CHILD):
        field = far_sum(leaf_far, leaf_coupling, window, base + n, lowest, CHILD)
        acc[pl.ds(n * leaf, leaf), :] += mm(turned[n], field.astype(BF16))
    skip = CHILD * rank

    def step(t, _):
        for b in range(BATCH):
            n = t * BATCH + b
            for r, held, low in ((0, tiles, 0), (1, other, base)):
                tile = work[3 * r, n]
                at = pl.multiple_of(skip + work[3 * r + 1, n] * leaf, rank)
                part = mm(held[low + tile // slots, lax.rem(tile, slots)], bulk2[pl.ds(at, leaf), :])
                acc[blocks(work[3 * r + 2, n], 1, leaf), :] += part
        return 0

    lax.fori_loop(0, work[6, 0], step, 0)
    stores = []
    for n in range(0, CHILD, 2):
        stores.append(
            pltpu.make_async_copy(acc.at[pl.ds(n * leaf, 2 * leaf)], out.at[blocks(base + n, 2, leaf)], sems.at[n // 2])
        )
        stores[-1].start()
    for store in stores:
        store.wait()


def shards(
    sources,
    near_tiles,
    near_index,
    near_count,
    leaf_basis,
    leaf_coupling,
    leaf_far,
    up_leaf,
    mid_coupling,
    mid_far,
    up_mid,
    top_coupling,
):
    sds = jax.ShapeDtypeStruct
    leaves, rank, leaf = leaf_basis.shape
    mids = up_leaf.shape[0]
    cols = sources.shape[1]
    slots = near_tiles.shape[1]
    total_top = top_coupling.shape[0]
    devices = lax.axis_size("leaf")
    group = CHILD // mids
    edge = CHILD * leaf
    edge_c = CHILD * rank
    rows = leaves * leaf
    assert leaves == 2 * CHILD and group >= 2 and total_top >= 4
    product_flops = 2 * leaf * leaf * cols

    rest = [(i, i + 1) for i in range(1, devices - 1, 2)]
    rest = rest + [(j, i) for i, j in rest]

    def swap(k):
        return [(i, i ^ k) for i in range(devices)]

    def send(x, pairs, axis="leaf"):
        return lax.ppermute(x, axis, pairs)

    def call(kernel, out_shape, in_specs, out_specs, scratch, mib, estimate, **more):
        def run(*args):
            return pl.pallas_call(
                kernel,
                out_shape=out_shape,
                in_specs=in_specs,
                out_specs=out_specs,
                scratch_shapes=scratch,
                compiler_params=params(mib),
                cost_estimate=estimate,
                **more,
            )(*args)

        return run

    index, count, far_index, mid_index = map(in_hbm, (near_index.T, near_count, leaf_far.T, mid_far))
    own_tiles = in_hbm(near_tiles)

    pack, bulk1, coef, src = call(
        upward,
        (
            sds(((mids + 1) * rank, cols), BF16),
            sds((edge_c + edge, cols), BF16),
            sds((leaves * rank, cols), BF16),
            sds((rows + leaf, cols), BF16),
        ),
        [HBM] * 4,
        (VMEM,) * 4,
        [
            pltpu.VMEM(leaf_basis.shape, BF16),
            pltpu.VMEM(up_leaf.shape, BF16),
            pltpu.VMEM(up_mid.shape, BF16),
            pltpu.SemaphoreType.DMA((2 * PARTS + 2,)),
        ],
        8,
        cost(2 * leaves * rank * leaf * cols, 4 << 20),
    )(*map(in_hbm, (sources, leaf_basis, up_leaf, up_mid)))
    src = in_vmem(src)

    pack1 = send(pack, swap(1))
    bulk1 = send(bulk1, swap(1))
    other = in_vmem(send(near_tiles, [(0, 1), (1, 0)], "col"))

    work, bulk2 = call(
        prepare,
        (sds((7, CHILD * slots + BATCH), jnp.int32), sds((edge_c + edge, cols), BF16)),
        [SMEM, SMEM, VMEM, VMEM],
        (SMEM, VMEM),
        [],
        8,
        cost(0, 4 << 20),
    )(index, count, coef, src)

    held = mids * rank
    plane = jnp.concatenate([pack[:held], pack1[:held]], axis=0)
    total = pack[held : held + rank].astype(F32) + pack1[held : held + rank].astype(F32)
    total = total.astype(BF16)
    k = 2
    while k < group:
        got = send(jnp.concatenate([plane, total], axis=0), swap(k))
        held = plane.shape[0]
        plane = jnp.concatenate([plane, got[:held]], axis=0)
        total = (total.astype(F32) + got[held:].astype(F32)).astype(BF16)
        k *= 2

    tops = [send(total, swap(k * group)) for k in range(1, total_top)]
    beyond = [(i, i + group) for i in range(group, devices - group) if i % (2 * group) >= group]
    next_a = send(plane, swap(group))
    next_b = send(plane, beyond + [(j, i) for i, j in beyond])
    bulk2 = send(bulk2, rest)

    half_tiles = (CHILD,) + near_tiles.shape[1:]
    near1, near2, tiles2 = call(
        near_most,
        (sds((edge, cols), F32), sds((edge, cols), F32), sds(half_tiles, BF16)),
        [SMEM, SMEM, HBM] + [VMEM] * 3,
        (VMEM,) * 3,
        [
            pltpu.VMEM(half_tiles, BF16),
            pltpu.VMEM((rows + edge + leaf, cols), BF16),
            pltpu.SemaphoreType.DMA((CHILD,)),
            pltpu.SemaphoreType.DMA((CHILD,)),
        ],
        20,
        cost(leaves * 2 * slots * product_flops, 16 << 20),
    )(index, count, own_tiles, other, src, bulk1)

    out, acc2, turned = call(
        downward,
        (sds((rows, cols), F32), sds((edge + leaf, cols), F32), sds((CHILD, leaf, rank), BF16)),
        [SMEM] * 2 + [VMEM] * (12 + total_top),
        (ANY, VMEM, VMEM),
        [
            pltpu.VMEM((edge, cols), F32),
            pltpu.VMEM((leaves * rank, cols), F32),
            pltpu.VMEM((edge_c + (leaves + 1) * rank, cols), BF16),
            pltpu.VMEM((mids * FAR * rank, cols), BF16),
            pltpu.VMEM((total_top * rank, cols), BF16),
            pltpu.SemaphoreType.DMA((CHILD // 2,)),
        ],
        16,
        cost(leaves * 4 * product_flops, 12 << 20),
    )(
        far_index, mid_index,
        near1, near2, coef, bulk1, plane, next_a, next_b,
        leaf_basis, leaf_coupling, up_leaf, mid_coupling, up_mid, top_coupling, *tops,
    )

    product, _ = call(
        near_last,
        (sds((rows, cols), F32), sds((edge + leaf, cols), F32)),
        [SMEM] * 2 + [VMEM] * 6 + [ANY],
        (ANY, VMEM),
        [pltpu.VMEM((edge_c + rank, cols), BF16), pltpu.SemaphoreType.DMA((CHILD // 2,))],
        8,
        cost(leaves * slots * product_flops, 4 << 20),
        input_output_aliases={8: 0, 5: 1},
    )(work, far_index, in_vmem(tiles2), other, bulk2, in_vmem(acc2), leaf_coupling, turned, out)
    return product


def solution(mesh):


    return jax.shard_map(
        shards,
        mesh=mesh,
        in_specs=(
            P("leaf", "col"),
            P("leaf", "col", None, None),
            P("leaf", None),
            P("leaf"),
            P("leaf", None, None),
            P("leaf", None, None),
            P("leaf", None),
            P("leaf", None, None),
            P("leaf", None, None),
            P("leaf", None),
            P("leaf", None, None),
            P(),
        ),
        out_specs=P("leaf", "col"),
        check_vma=False,
    )
```

```python
import jax
import jax.numpy as jnp
from jax import lax
from jax.experimental import pallas as pl
from jax.experimental.pallas import tpu as pltpu
from jax.sharding import PartitionSpec as P


CHILD = 8
FAR = 4
BATCH = 4
PARTS = 4

F32 = jnp.float32
BF16 = jnp.bfloat16
VMEM = pl.BlockSpec(memory_space=pltpu.VMEM)
SMEM = pl.BlockSpec(memory_space=pltpu.SMEM)
HBM = pl.BlockSpec(memory_space=pltpu.HBM)
ANY = pl.BlockSpec(memory_space=pl.ANY)


def mm(a, b):
    return jnp.dot(a, b, preferred_element_type=F32)


def mm_t(a, b):
    return lax.dot_general(a, b, (((0,), (0,)), ((), ())), preferred_element_type=F32)


def cost(flops, nbytes):
    return pl.CostEstimate(flops=flops, transcendentals=0, bytes_accessed=nbytes)


def params(mib):
    return pltpu.CompilerParams(vmem_limit_bytes=mib << 20)


def in_vmem(x):
    return pltpu.with_memory_space_constraint(x, pltpu.VMEM)


def in_hbm(x):
    return pltpu.with_memory_space_constraint(x, pltpu.HBM)


def blocks(start, count, size):
    return pl.ds(pl.multiple_of(start * size, size), count * size)


def upward(
    src_hbm, basis_hbm, up_leaf_hbm, up_mid_hbm,
    pack, bulk1, coef, src,
    basis, up_leaf, up_mid, sems,
):
    leaves, rank, leaf = basis.shape
    mids = up_leaf.shape[0]
    step = leaves // PARTS
    loads = []
    for p in range(PARTS):
        near = pl.ds(p * step * leaf, step * leaf)
        far = pl.ds(p * step, step)
        loads.append(pltpu.make_async_copy(src_hbm.at[near], src.at[near], sems.at[2 * p]))
        loads.append(pltpu.make_async_copy(basis_hbm.at[far], basis.at[far], sems.at[2 * p + 1]))
    loads.append(pltpu.make_async_copy(up_leaf_hbm, up_leaf, sems.at[2 * PARTS]))
    loads.append(pltpu.make_async_copy(up_mid_hbm, up_mid, sems.at[2 * PARTS + 1]))
    for load in loads:
        load.start()
    src[pl.ds(leaves * leaf, leaf), :] = jnp.zeros((leaf, src.shape[1]), BF16)
    odd = lax.rem(lax.axis_index("leaf"), 2)
    for p in range(PARTS):
        loads[2 * p].wait()
        loads[2 * p + 1].wait()
        for i in range(p * step, (p + 1) * step):
            coef[pl.ds(i * rank, rank), :] = mm(basis[i], src[pl.ds(i * leaf, leaf), :]).astype(BF16)
    first = (1 - odd) * (leaves - CHILD)
    bulk1[pl.ds(0, CHILD * rank), :] = coef[blocks(first, CHILD, rank), :]
    bulk1[pl.ds(CHILD * rank, CHILD * leaf), :] = src[blocks(first, CHILD, leaf), :]
    loads[2 * PARTS].wait()
    loads[2 * PARTS + 1].wait()
    total = None
    for q in range(mids):
        mid = mm(up_leaf[q], coef[pl.ds(q * CHILD * rank, CHILD * rank), :]).astype(BF16)
        pack[pl.ds(q * rank, rank), :] = mid
        lift = mm(up_mid[q], mid).astype(BF16).astype(F32)
        total = lift if total is None else total + lift
    pack[pl.ds(mids * rank, rank), :] = total.astype(BF16)


def prepare(index, count, leaf_far, coef, src, work, bulk2):
    leaves = index.shape[1]
    slots = index.shape[0] // 2
    rank = coef.shape[0] // leaves
    leaf = src.shape[0] // (leaves + 1)
    device = lax.axis_index("leaf")
    odd = lax.rem(device, 2)
    core = lax.axis_index("col")
    base = odd * (leaves - CHILD)
    bulk2[pl.ds(0, CHILD * rank), :] = coef[blocks(base, CHILD, rank), :]
    bulk2[pl.ds(CHILD * rank, CHILD * leaf), :] = src[blocks(base, CHILD, leaf), :]
    lowest = jnp.where(odd == 1, leaves, -CHILD) + device * leaves

    room = work.shape[1] // 2
    for part in range(2):
        start = jnp.bitwise_xor(part, odd) * (CHILD // 2)

        def row(t, found):
            n = start + t
            live = count[base + n]
            for f in range(FAR):
                at = leaf_far[f, base + n] - lowest
                work[7 + f, n] = jnp.where((at >= 0) & (at < CHILD), at, CHILD)
            out = []
            for r, owner in ((0, core), (1, 1 - core)):
                at = found[r]
                for k in range(slots):
                    slot = owner * slots + k
                    outside = index[slot, base + n] - lowest
                    work[3 * r, at] = n * slots + k
                    work[3 * r + 1, at] = outside
                    work[3 * r + 2, at] = n
                    use = (slot < live) & (outside >= 0) & (outside < CHILD)
                    at = at + use.astype(jnp.int32)
                out.append(at)
            return tuple(out)

        begin = jnp.int32(part * room)
        found = lax.fori_loop(0, CHILD // 2, row, (begin, begin))
        rounds = (jnp.maximum(found[0], found[1]) - begin + BATCH - 1) // BATCH
        work[6, part] = rounds
        for r in range(2):

            def fill(n, _):
                work[3 * r, n] = 0
                work[3 * r + 1, n] = 0
                work[3 * r + 2, n] = CHILD
                return 0

            lax.fori_loop(found[r], begin + rounds * BATCH, fill, 0)


def fold(basis_hbm, coupling_hbm, folded, basis, coupling, sems):
    leaves = basis_hbm.shape[0]
    base = lax.rem(lax.axis_index("leaf"), 2) * (leaves - CHILD)
    loads = [
        pltpu.make_async_copy(a.at[pl.ds(base, CHILD)], b, sems.at[k])
        for k, (a, b) in enumerate(((basis_hbm, basis), (coupling_hbm, coupling)))
    ]
    for load in loads:
        load.start()
    for load in loads:
        load.wait()
    for n in range(CHILD):
        folded[n] = mm_t(basis[n], coupling[n]).astype(BF16)


def join(pack, pack1, pair, part):
    held = part.shape[0]
    mids = pack.shape[0] - held
    total = pack[pl.ds(mids, held), :].astype(F32) + pack1[pl.ds(mids, held), :].astype(F32)
    pair[pl.ds(0, mids), :] = pack[pl.ds(0, mids), :]
    pair[pl.ds(mids, mids), :] = pack1[pl.ds(0, mids), :]
    pair[pl.ds(2 * mids, held), :] = total.astype(BF16)
    part[...] = total.astype(BF16)


def cluster(pair, pair1, plane):
    mids = plane.shape[0] - pair.shape[0]
    held = pair.shape[0] - mids
    plane[pl.ds(0, mids), :] = pair[pl.ds(0, mids), :]
    plane[pl.ds(mids, mids), :] = pair1[pl.ds(0, mids), :]
    total = pair[pl.ds(mids, held), :].astype(F32) + pair1[pl.ds(mids, held), :].astype(F32)
    plane[pl.ds(2 * mids, held), :] = total.astype(BF16)


def stacked(*refs):
    out = refs[-1]
    held = refs[0].shape[0]
    for k, part in enumerate(refs[:-1]):
        out[pl.ds(k * held, held), :] = part[...]


def load_tiles(tiles_hbm, tiles, sems, base):
    loads = [
        pltpu.make_async_copy(tiles_hbm.at[base + n], tiles.at[n], sems.at[n])
        for n in range(tiles.shape[0])
    ]
    for load in loads:
        load.start()
    return loads


def product(index, live, held, n, k, slot, i, window, lowest, total):
    leaf = held.shape[3]
    at = index[slot, i] - lowest
    place = jnp.where((slot < live) & (at >= 0) & (at < total), at, total)
    return mm(held[n, k], window[blocks(place, 1, leaf), :])


def near_most(index, count, tiles_hbm, other, src, bulk1, acc1, acc2, tiles2, tiles1, window, sems1, sems2):
    leaves, slots, leaf, _ = other.shape
    device = lax.axis_index("leaf")
    odd = lax.rem(device, 2)
    core = lax.axis_index("col")
    base1 = (1 - odd) * (leaves - CHILD)
    base2 = odd * (leaves - CHILD)
    loads2 = load_tiles(tiles_hbm, tiles2, sems2, base2)
    loads1 = load_tiles(tiles_hbm, tiles1, sems1, base1)
    total = leaves + CHILD
    window[blocks(odd * CHILD, leaves, leaf), :] = src[pl.ds(0, leaves * leaf), :]
    window[blocks((1 - odd) * leaves, CHILD, leaf), :] = bulk1[pl.ds(bulk1.shape[0] - CHILD * leaf, CHILD * leaf), :]
    window[pl.ds(total * leaf, leaf), :] = jnp.zeros((leaf, src.shape[1]), BF16)
    lowest = device * leaves - odd * CHILD

    def others2(n, _):
        i = base2 + n
        acc2[blocks(n, 1, leaf), :] = sum(
            product(index, count[i], other, i, k, (1 - core) * slots + k, i, src, device * leaves, leaves)
            for k in range(slots)
        )
        return 0

    lax.fori_loop(0, CHILD, others2, 0, unroll=4)
    for load in loads2:
        load.wait()

    def own2(n, _):
        i = base2 + n
        acc2[blocks(n, 1, leaf), :] += sum(
            product(index, count[i], tiles2, n, k, core * slots + k, i, src, device * leaves, leaves)
            for k in range(slots)
        )
        return 0

    lax.fori_loop(0, CHILD, own2, 0, unroll=4)
    for load in loads1:
        load.wait()

    def all1(n, _):
        i = base1 + n
        acc1[blocks(n, 1, leaf), :] = sum(
            product(index, count[i], held, at, k, owner * slots + k, i, window, lowest, total)
            for held, at, owner in ((tiles1, n, core), (other, i, 1 - core))
            for k in range(slots)
        )
        return 0

    lax.fori_loop(0, CHILD, all1, 0, unroll=2)


def downward(
    leaf_far, mid_far,
    near1, near2, coef, bulk1, plane, next_a, next_b, beyond0, beyond1,
    basis, leaf_coupling, up_leaf, mid_coupling, up_mid, top_coupling,
    out, acc2,
    full, down, window, chosen, stack, sems,
):
    total_top = top_coupling.shape[0]
    leaves, rank, leaf = basis.shape
    mids = up_leaf.shape[0]
    group = CHILD // mids
    device = lax.axis_index("leaf")
    odd = lax.rem(device, 2)
    parent = device // group
    member = lax.rem(device, group)

    stack[blocks(parent, 1, rank), :] = jnp.zeros((rank, full.shape[1]), BF16)
    stack[blocks(jnp.bitwise_xor(parent, 1), 1, rank), :] = next_a[pl.ds(CHILD * rank, rank), :]
    for p in range(2, total_top):
        rows = pl.ds((p - 2) * rank, rank)
        top = beyond0[rows, :].astype(F32) + beyond1[rows, :].astype(F32)
        stack[blocks(jnp.bitwise_xor(parent, p), 1, rank), :] = top.astype(BF16)
    top_field = mm(top_coupling[parent], stack[...]).astype(BF16)

    total = leaves + CHILD
    lowest = device * leaves - odd * CHILD
    window[blocks(odd * CHILD, leaves, rank), :] = coef[...]
    window[blocks((1 - odd) * leaves, CHILD, rank), :] = bulk1[pl.ds(0, CHILD * rank), :]
    window[pl.ds(total * rank, rank), :] = jnp.zeros((rank, full.shape[1]), BF16)

    for q in range(mids):
        for f in range(FAR):
            b = mid_far[q, f]
            above = b // CHILD
            inside = lax.rem(b, CHILD)
            place = jnp.bitwise_xor(inside // mids, member) * mids + lax.rem(inside, mids)
            row = blocks(place, 1, rank)
            to = pl.ds((q * FAR + f) * rank, rank)
            beside = jnp.bitwise_xor(parent, 1)

            @pl.when(above == parent)
            def _():
                chosen[to, :] = plane[row, :]

            @pl.when(above == beside)
            def _():
                chosen[to, :] = next_a[row, :]

            @pl.when((above != parent) & (above != beside))
            def _():
                chosen[to, :] = next_b[row, :]

    for q in range(mids):
        picked = chosen[pl.ds(q * FAR * rank, FAR * rank), :]
        mid_field = (mm(mid_coupling[q], picked) + mm_t(up_mid[q], top_field)).astype(BF16)
        down[pl.ds(q * CHILD * rank, CHILD * rank), :] = mm_t(up_leaf[q], mid_field)

    def field_of(i):
        field = far_sum(leaf_far, leaf_coupling, window, i, lowest, total)
        return (field + down[blocks(i, 1, rank), :]).astype(BF16)

    base1 = (1 - odd) * (leaves - CHILD)
    base2 = odd * (leaves - CHILD)
    stores = []
    for n in range(CHILD):
        rows = pl.ds(n * leaf, leaf)
        full[rows, :] = near1[rows, :] + mm_t(basis[base1 + n], field_of(base1 + n))
        if n % 2 == 1:
            rows = pl.ds((n - 1) * leaf, 2 * leaf)
            stores.append(
                pltpu.make_async_copy(full.at[rows], out.at[blocks(base1 + n - 1, 2, leaf)], sems.at[n // 2])
            )
            stores[-1].start()
    for n in range(CHILD):
        rows = pl.ds(n * leaf, leaf)
        acc2[rows, :] = near2[rows, :] + mm_t(basis[base2 + n], field_of(base2 + n))
    for store in stores:
        store.wait()


def far_sum(leaf_far, leaf_coupling, window, i, lowest, total):
    rank = leaf_coupling.shape[1]
    picked = []
    for f in range(FAR):
        at = leaf_far[f, i] - lowest
        place = jnp.where((at >= 0) & (at < total), at, total)
        picked.append(window[blocks(place, 1, rank), :])
    return mm(leaf_coupling[i], jnp.concatenate(picked, axis=0))


def near_last(work, tiles, other, bulk2, acc_in, folded, out_in, out, acc, window, sems):
    leaves, slots, leaf, _ = other.shape
    rank = window.shape[0] // (CHILD + 1)
    odd = lax.rem(lax.axis_index("leaf"), 2)
    base = odd * (leaves - CHILD)
    window[pl.ds(0, CHILD * rank), :] = bulk2[pl.ds(0, CHILD * rank), :]
    window[pl.ds(CHILD * rank, rank), :] = jnp.zeros((rank, bulk2.shape[1]), BF16)
    skip = CHILD * rank
    room = work.shape[1] // 2
    count = CHILD // 2
    stores = []
    for half in range(2):
        start = jnp.bitwise_xor(half, odd) * count
        for t in range(count):
            n = start + t
            picked = [window[blocks(work[7 + f, n], 1, rank), :] for f in range(FAR)]
            acc[blocks(n, 1, leaf), :] += mm(folded[n], jnp.concatenate(picked, axis=0))

        def step(t, _):
            for b in range(BATCH):
                n = half * room + t * BATCH + b
                for r, held, low in ((0, tiles, 0), (1, other, base)):
                    tile = work[3 * r, n]
                    at = pl.multiple_of(skip + work[3 * r + 1, n] * leaf, rank)
                    part = mm(held[low + tile // slots, lax.rem(tile, slots)], bulk2[pl.ds(at, leaf), :])
                    acc[blocks(work[3 * r + 2, n], 1, leaf), :] += part
            return 0

        lax.fori_loop(0, work[6, half], step, 0)
        stores.append(
            pltpu.make_async_copy(acc.at[blocks(start, count, leaf)], out.at[blocks(base + start, count, leaf)], sems.at[half])
        )
        stores[-1].start()
    for store in stores:
        store.wait()


def shards(
    sources,
    near_tiles,
    near_index,
    near_count,
    leaf_basis,
    leaf_coupling,
    leaf_far,
    up_leaf,
    mid_coupling,
    mid_far,
    up_mid,
    top_coupling,
):
    sds = jax.ShapeDtypeStruct
    leaves, rank, leaf = leaf_basis.shape
    mids = up_leaf.shape[0]
    cols = sources.shape[1]
    slots = near_tiles.shape[1]
    total_top = top_coupling.shape[0]
    devices = lax.axis_size("leaf")
    group = CHILD // mids
    edge = CHILD * leaf
    edge_c = CHILD * rank
    rows = leaves * leaf
    assert leaves == 2 * CHILD and group == 4 and total_top >= 4
    product_flops = 2 * leaf * leaf * cols

    rest = [(i, i + 1) for i in range(1, devices - 1, 2)]
    rest = rest + [(j, i) for i, j in rest]

    def swap(k):
        return [(i, i ^ k) for i in range(devices)]

    def send(x, pairs, axis="leaf"):
        return lax.ppermute(x, axis, pairs)

    def call(kernel, out_shape, in_specs, out_specs, scratch, mib, estimate, **more):
        def run(*args):
            return pl.pallas_call(
                kernel,
                out_shape=out_shape,
                in_specs=in_specs,
                out_specs=out_specs,
                scratch_shapes=scratch,
                compiler_params=params(mib),
                cost_estimate=estimate,
                **more,
            )(*args)

        return run

    index, count, far_index, mid_index = map(in_hbm, (near_index.T, near_count, leaf_far.T, mid_far))
    own_tiles = in_hbm(near_tiles)

    pack, bulk1, coef, src = call(
        upward,
        (
            sds(((mids + 1) * rank, cols), BF16),
            sds((edge_c + edge, cols), BF16),
            sds((leaves * rank, cols), BF16),
            sds((rows + leaf, cols), BF16),
        ),
        [HBM] * 4,
        (VMEM,) * 4,
        [
            pltpu.VMEM(leaf_basis.shape, BF16),
            pltpu.VMEM(up_leaf.shape, BF16),
            pltpu.VMEM(up_mid.shape, BF16),
            pltpu.SemaphoreType.DMA((2 * PARTS + 2,)),
        ],
        8,
        cost(2 * leaves * rank * leaf * cols, 4 << 20),
    )(*map(in_hbm, (sources, leaf_basis, up_leaf, up_mid)))
    src = in_vmem(src)

    pack1 = send(pack, swap(1))
    bulk1 = send(bulk1, swap(1))
    other = in_vmem(send(near_tiles, [(0, 1), (1, 0)], "col"))

    work, bulk2 = call(
        prepare,
        (sds((7 + FAR, CHILD * slots + 2 * BATCH), jnp.int32), sds((edge_c + edge, cols), BF16)),
        [SMEM, SMEM, SMEM, VMEM, VMEM],
        (SMEM, VMEM),
        [],
        8,
        cost(0, 4 << 20),
    )(index, count, far_index, coef, src)

    held = mids * rank
    pair, part = call(
        join,
        (sds((2 * held + rank, cols), BF16), sds((rank, cols), BF16)),
        [VMEM] * 2,
        (VMEM,) * 2,
        [],
        4,
        cost(0, 1 << 18),
    )(pack, pack1)

    pair1 = send(pair, swap(2))
    parts = [send(part, swap(k * group)) for k in range(2, total_top)]
    plane = call(
        cluster,
        sds((4 * held + rank, cols), BF16),
        [VMEM] * 2,
        VMEM,
        [],
        4,
        cost(0, 1 << 18),
    )(pair, pair1)
    beyond = call(
        stacked,
        sds(((total_top - 2) * rank, cols), BF16),
        [VMEM] * len(parts),
        VMEM,
        [],
        4,
        cost(0, 1 << 18),
    )(*parts)
    next_pairs = [(i, i + group) for i in range(group, devices - group) if i % (2 * group) >= group]
    next_a = send(plane, swap(group))
    next_b = send(plane, next_pairs + [(j, i) for i, j in next_pairs])
    beyond1 = send(beyond, swap(2))
    bulk2 = send(bulk2, rest)

    folded = call(
        fold,
        sds((CHILD, leaf, leaf_coupling.shape[2]), BF16),
        [HBM] * 2,
        VMEM,
        [
            pltpu.VMEM((CHILD,) + leaf_basis.shape[1:], BF16),
            pltpu.VMEM((CHILD,) + leaf_coupling.shape[1:], BF16),
            pltpu.SemaphoreType.DMA((2,)),
        ],
        6,
        cost(CHILD * 2 * leaf * leaf * rank, 2 << 20),
    )(in_hbm(leaf_basis), in_hbm(leaf_coupling))

    half_tiles = (CHILD,) + near_tiles.shape[1:]
    near1, near2, tiles2 = call(
        near_most,
        (sds((edge, cols), F32), sds((edge, cols), F32), sds(half_tiles, BF16)),
        [SMEM, SMEM, HBM] + [VMEM] * 3,
        (VMEM,) * 3,
        [
            pltpu.VMEM(half_tiles, BF16),
            pltpu.VMEM((rows + edge + leaf, cols), BF16),
            pltpu.SemaphoreType.DMA((CHILD,)),
            pltpu.SemaphoreType.DMA((CHILD,)),
        ],
        20,
        cost(leaves * 2 * slots * product_flops, 16 << 20),
    )(index, count, own_tiles, other, src, bulk1)

    out, acc2 = call(
        downward,
        (sds((rows, cols), F32), sds((edge + leaf, cols), F32)),
        [SMEM] * 2 + [VMEM] * 15,
        (ANY, VMEM),
        [
            pltpu.VMEM((edge, cols), F32),
            pltpu.VMEM((leaves * rank, cols), F32),
            pltpu.VMEM((edge_c + (leaves + 1) * rank, cols), BF16),
            pltpu.VMEM((mids * FAR * rank, cols), BF16),
            pltpu.VMEM((total_top * rank, cols), BF16),
            pltpu.SemaphoreType.DMA((CHILD // 2,)),
        ],
        16,
        cost(leaves * 4 * product_flops, 12 << 20),
    )(
        far_index, mid_index,
        near1, near2, coef, bulk1, plane, next_a, next_b, beyond, beyond1,
        leaf_basis, leaf_coupling, up_leaf, mid_coupling, up_mid, top_coupling,
    )

    product, _ = call(
        near_last,
        (sds((rows, cols), F32), sds((edge + leaf, cols), F32)),
        [SMEM] + [VMEM] * 5 + [ANY],
        (ANY, VMEM),
        [pltpu.VMEM((edge_c + rank, cols), BF16), pltpu.SemaphoreType.DMA((2,))],
        8,
        cost(leaves * slots * product_flops, 4 << 20),
        input_output_aliases={6: 0, 4: 1},
    )(work, in_vmem(tiles2), other, bulk2, in_vmem(acc2), folded, out)
    return product


def solution(mesh):


    return jax.shard_map(
        shards,
        mesh=mesh,
        in_specs=(
            P("leaf", "col"),
            P("leaf", "col", None, None),
            P("leaf", None),
            P("leaf"),
            P("leaf", None, None),
            P("leaf", None, None),
            P("leaf", None),
            P("leaf", None, None),
            P("leaf", None, None),
            P("leaf", None),
            P("leaf", None, None),
            P(),
        ),
        out_specs=P("leaf", "col"),
        check_vma=False,
    )
```

```python
import functools

import jax
import jax.numpy as jnp
from jax import lax
from jax.experimental import pallas as pl
from jax.experimental.pallas import tpu as pltpu
from jax.sharding import PartitionSpec as P


CHILD = 8
FAR = 4
BATCH = 4
PARTS = 2

F32 = jnp.float32
BF16 = jnp.bfloat16
VMEM = pl.BlockSpec(memory_space=pltpu.VMEM)
SMEM = pl.BlockSpec(memory_space=pltpu.SMEM)
HBM = pl.BlockSpec(memory_space=pltpu.HBM)
ANY = pl.BlockSpec(memory_space=pl.ANY)


def mm(a, b):
    return jnp.dot(a, b, preferred_element_type=F32)


def mm_t(a, b):
    return lax.dot_general(a, b, (((0,), (0,)), ((), ())), preferred_element_type=F32)


def cost(flops, nbytes):
    return pl.CostEstimate(flops=flops, transcendentals=0, bytes_accessed=nbytes)


def params(mib):
    return pltpu.CompilerParams(vmem_limit_bytes=mib << 20)


def in_vmem(x):
    return pltpu.with_memory_space_constraint(x, pltpu.VMEM)


def in_hbm(x):
    return pltpu.with_memory_space_constraint(x, pltpu.HBM)


def blocks(start, count, size):
    return pl.ds(pl.multiple_of(start * size, size), count * size)


def upward(
    src_hbm, basis_hbm, up_leaf_hbm, up_mid_hbm,
    pack, bulk1, coef, src,
    basis, up_leaf, up_mid, sems,
):
    leaves, rank, leaf = basis.shape
    mids = up_leaf.shape[0]
    step = leaves // PARTS
    loads = []
    for p in range(PARTS):
        near = pl.ds(p * step * leaf, step * leaf)
        far = pl.ds(p * step, step)
        loads.append(pltpu.make_async_copy(src_hbm.at[near], src.at[near], sems.at[2 * p]))
        loads.append(pltpu.make_async_copy(basis_hbm.at[far], basis.at[far], sems.at[2 * p + 1]))
    loads.append(pltpu.make_async_copy(up_leaf_hbm, up_leaf, sems.at[2 * PARTS]))
    loads.append(pltpu.make_async_copy(up_mid_hbm, up_mid, sems.at[2 * PARTS + 1]))
    for load in loads:
        load.start()
    src[pl.ds(leaves * leaf, leaf), :] = jnp.zeros((leaf, src.shape[1]), BF16)
    odd = lax.rem(lax.axis_index("leaf"), 2)
    for p in range(PARTS):
        loads[2 * p].wait()
        loads[2 * p + 1].wait()
        for i in range(p * step, (p + 1) * step):
            coef[pl.ds(i * rank, rank), :] = mm(basis[i], src[pl.ds(i * leaf, leaf), :]).astype(BF16)
    first = (1 - odd) * (leaves - CHILD)
    bulk1[pl.ds(0, CHILD * rank), :] = coef[blocks(first, CHILD, rank), :]
    bulk1[pl.ds(CHILD * rank, CHILD * leaf), :] = src[blocks(first, CHILD, leaf), :]
    loads[2 * PARTS].wait()
    loads[2 * PARTS + 1].wait()
    total = None
    for q in range(mids):
        mid = mm(up_leaf[q], coef[pl.ds(q * CHILD * rank, CHILD * rank), :]).astype(BF16)
        pack[pl.ds(q * rank, rank), :] = mid
        lift = mm(up_mid[q], mid).astype(BF16).astype(F32)
        total = lift if total is None else total + lift
    pack[pl.ds(mids * rank, rank), :] = total.astype(BF16)


def prepare(index, count, leaf_far, coef, src, work, bulk2):
    leaves = index.shape[1]
    slots = index.shape[0] // 2
    rank = coef.shape[0] // leaves
    leaf = src.shape[0] // (leaves + 1)
    device = lax.axis_index("leaf")
    odd = lax.rem(device, 2)
    core = lax.axis_index("col")
    base = odd * (leaves - CHILD)
    bulk2[pl.ds(0, CHILD * rank), :] = coef[blocks(base, CHILD, rank), :]
    bulk2[pl.ds(CHILD * rank, CHILD * leaf), :] = src[blocks(base, CHILD, leaf), :]
    lowest = jnp.where(odd == 1, leaves, -CHILD) + device * leaves

    room = work.shape[1] // 2
    for part in range(2):
        start = jnp.bitwise_xor(part, odd) * (CHILD // 2)

        def row(t, found):
            n = start + t
            live = count[base + n]
            for f in range(FAR):
                at = leaf_far[f, base + n] - lowest
                work[7 + f, n] = jnp.where((at >= 0) & (at < CHILD), at, CHILD)
            out = []
            for r, owner in ((0, core), (1, 1 - core)):
                at = found[r]
                for k in range(slots):
                    slot = owner * slots + k
                    outside = index[slot, base + n] - lowest
                    work[3 * r, at] = n * slots + k
                    work[3 * r + 1, at] = outside
                    work[3 * r + 2, at] = n
                    use = (slot < live) & (outside >= 0) & (outside < CHILD)
                    at = at + use.astype(jnp.int32)
                out.append(at)
            return tuple(out)

        begin = jnp.int32(part * room)
        found = lax.fori_loop(0, CHILD // 2, row, (begin, begin))
        rounds = (jnp.maximum(found[0], found[1]) - begin + BATCH - 1) // BATCH
        work[6, part] = rounds
        for r in range(2):

            def fill(n, _):
                work[3 * r, n] = 0
                work[3 * r + 1, n] = 0
                work[3 * r + 2, n] = CHILD
                return 0

            lax.fori_loop(found[r], begin + rounds * BATCH, fill, 0)


def fold(late, last, basis_hbm, coupling_hbm, *refs):
    folded, basis, coupling, sems = refs[-4:]
    leaves, _, _ = basis_hbm.shape
    device = lax.axis_index("leaf")
    base = lax.rem(device, 2) * (leaves - CHILD)

    @pl.when((device >= last) == late)
    def _():
        loads = [
            pltpu.make_async_copy(a.at[pl.ds(base, CHILD)], b, sems.at[k])
            for k, (a, b) in enumerate(((basis_hbm, basis), (coupling_hbm, coupling)))
        ]
        for load in loads:
            load.start()
        for load in loads:
            load.wait()
        for n in range(CHILD):
            folded[n] = mm_t(basis[n], coupling[n]).astype(BF16)


def join(pack, pack1, pair, part):
    held = part.shape[0]
    mids = pack.shape[0] - held
    total = pack[pl.ds(mids, held), :].astype(F32) + pack1[pl.ds(mids, held), :].astype(F32)
    pair[pl.ds(0, mids), :] = pack[pl.ds(0, mids), :]
    pair[pl.ds(mids, mids), :] = pack1[pl.ds(0, mids), :]
    pair[pl.ds(2 * mids, held), :] = total.astype(BF16)
    part[...] = total.astype(BF16)


def cluster(pair, pair1, plane):
    mids = plane.shape[0] - pair.shape[0]
    held = pair.shape[0] - mids
    plane[pl.ds(0, mids), :] = pair[pl.ds(0, mids), :]
    plane[pl.ds(mids, mids), :] = pair1[pl.ds(0, mids), :]
    total = pair[pl.ds(mids, held), :].astype(F32) + pair1[pl.ds(mids, held), :].astype(F32)
    plane[pl.ds(2 * mids, held), :] = total.astype(BF16)


def stacked(*refs):
    out = refs[-1]
    held = refs[0].shape[0]
    for k, part in enumerate(refs[:-1]):
        out[pl.ds(k * held, held), :] = part[...]


def load_tiles(tiles_hbm, tiles, sems, base):
    loads = [
        pltpu.make_async_copy(tiles_hbm.at[base + n], tiles.at[n], sems.at[n])
        for n in range(tiles.shape[0])
    ]
    for load in loads:
        load.start()
    return loads


def product(index, live, held, n, k, slot, i, window, lowest, total):
    leaf = held.shape[3]
    at = index[slot, i] - lowest
    place = jnp.where((slot < live) & (at >= 0) & (at < total), at, total)
    return mm(held[n, k], window[blocks(place, 1, leaf), :])


def near_most(index, count, tiles_hbm, other, src, bulk1, acc1, acc2, tiles2, tiles1, window, sems1, sems2):
    leaves, slots, leaf, _ = other.shape
    device = lax.axis_index("leaf")
    odd = lax.rem(device, 2)
    core = lax.axis_index("col")
    base1 = (1 - odd) * (leaves - CHILD)
    base2 = odd * (leaves - CHILD)
    loads2 = load_tiles(tiles_hbm, tiles2, sems2, base2)
    loads1 = load_tiles(tiles_hbm, tiles1, sems1, base1)
    total = leaves + CHILD
    window[blocks(odd * CHILD, leaves, leaf), :] = src[pl.ds(0, leaves * leaf), :]
    window[blocks((1 - odd) * leaves, CHILD, leaf), :] = bulk1[pl.ds(bulk1.shape[0] - CHILD * leaf, CHILD * leaf), :]
    window[pl.ds(total * leaf, leaf), :] = jnp.zeros((leaf, src.shape[1]), BF16)
    lowest = device * leaves - odd * CHILD

    def others2(n, _):
        i = base2 + n
        acc2[blocks(n, 1, leaf), :] = sum(
            product(index, count[i], other, i, k, (1 - core) * slots + k, i, src, device * leaves, leaves)
            for k in range(slots)
        )
        return 0

    lax.fori_loop(0, CHILD, others2, 0, unroll=4)
    for load in loads2:
        load.wait()

    def own2(n, _):
        i = base2 + n
        acc2[blocks(n, 1, leaf), :] += sum(
            product(index, count[i], tiles2, n, k, core * slots + k, i, src, device * leaves, leaves)
            for k in range(slots)
        )
        return 0

    lax.fori_loop(0, CHILD, own2, 0, unroll=4)
    for load in loads1:
        load.wait()

    def all1(n, _):
        i = base1 + n
        acc1[blocks(n, 1, leaf), :] = sum(
            product(index, count[i], held, at, k, owner * slots + k, i, window, lowest, total)
            for held, at, owner in ((tiles1, n, core), (other, i, 1 - core))
            for k in range(slots)
        )
        return 0

    lax.fori_loop(0, CHILD, all1, 0, unroll=2)


def downward(
    leaf_far, mid_far,
    near1, near2, coef, bulk1, plane, next_a, next_b, beyond0, beyond1,
    basis, leaf_coupling, up_leaf, mid_coupling, up_mid, top_coupling,
    out, acc2,
    full, down, window, chosen, stack, sems,
):
    total_top = top_coupling.shape[0]
    leaves, rank, leaf = basis.shape
    mids = up_leaf.shape[0]
    group = CHILD // mids
    device = lax.axis_index("leaf")
    odd = lax.rem(device, 2)
    parent = device // group
    member = lax.rem(device, group)

    stack[blocks(parent, 1, rank), :] = jnp.zeros((rank, full.shape[1]), BF16)
    stack[blocks(jnp.bitwise_xor(parent, 1), 1, rank), :] = next_a[pl.ds(CHILD * rank, rank), :]
    for p in range(2, total_top):
        rows = pl.ds((p - 2) * rank, rank)
        top = beyond0[rows, :].astype(F32) + beyond1[rows, :].astype(F32)
        stack[blocks(jnp.bitwise_xor(parent, p), 1, rank), :] = top.astype(BF16)
    top_field = mm(top_coupling[parent], stack[...]).astype(BF16)

    total = leaves + CHILD
    lowest = device * leaves - odd * CHILD
    window[blocks(odd * CHILD, leaves, rank), :] = coef[...]
    window[blocks((1 - odd) * leaves, CHILD, rank), :] = bulk1[pl.ds(0, CHILD * rank), :]
    window[pl.ds(total * rank, rank), :] = jnp.zeros((rank, full.shape[1]), BF16)

    for q in range(mids):
        for f in range(FAR):
            b = mid_far[q, f]
            above = b // CHILD
            inside = lax.rem(b, CHILD)
            place = jnp.bitwise_xor(inside // mids, member) * mids + lax.rem(inside, mids)
            row = blocks(place, 1, rank)
            to = pl.ds((q * FAR + f) * rank, rank)
            beside = jnp.bitwise_xor(parent, 1)

            @pl.when(above == parent)
            def _():
                chosen[to, :] = plane[row, :]

            @pl.when(above == beside)
            def _():
                chosen[to, :] = next_a[row, :]

            @pl.when((above != parent) & (above != beside))
            def _():
                chosen[to, :] = next_b[row, :]

    for q in range(mids):
        picked = chosen[pl.ds(q * FAR * rank, FAR * rank), :]
        mid_field = (mm(mid_coupling[q], picked) + mm_t(up_mid[q], top_field)).astype(BF16)
        down[pl.ds(q * CHILD * rank, CHILD * rank), :] = mm_t(up_leaf[q], mid_field)

    def field_of(i):
        field = far_sum(leaf_far, leaf_coupling, window, i, lowest, total)
        return (field + down[blocks(i, 1, rank), :]).astype(BF16)

    base1 = (1 - odd) * (leaves - CHILD)
    base2 = odd * (leaves - CHILD)
    stores = []
    for n in range(CHILD):
        rows = pl.ds(n * leaf, leaf)
        full[rows, :] = near1[rows, :] + mm_t(basis[base1 + n], field_of(base1 + n))
        if n % 2 == 1:
            rows = pl.ds((n - 1) * leaf, 2 * leaf)
            stores.append(
                pltpu.make_async_copy(full.at[rows], out.at[blocks(base1 + n - 1, 2, leaf)], sems.at[n // 2])
            )
            stores[-1].start()
    for n in range(CHILD):
        rows = pl.ds(n * leaf, leaf)
        acc2[rows, :] = near2[rows, :] + mm_t(basis[base2 + n], field_of(base2 + n))
    for store in stores:
        store.wait()


def far_sum(leaf_far, leaf_coupling, window, i, lowest, total):
    rank = leaf_coupling.shape[1]
    picked = []
    for f in range(FAR):
        at = leaf_far[f, i] - lowest
        place = jnp.where((at >= 0) & (at < total), at, total)
        picked.append(window[blocks(place, 1, rank), :])
    return mm(leaf_coupling[i], jnp.concatenate(picked, axis=0))


def near_last(work, tiles, other, bulk2, acc_in, folded, out_in, out, acc, window, sems):
    leaves, slots, leaf, _ = other.shape
    rank = window.shape[0] // (CHILD + 1)
    odd = lax.rem(lax.axis_index("leaf"), 2)
    base = odd * (leaves - CHILD)
    window[pl.ds(0, CHILD * rank), :] = bulk2[pl.ds(0, CHILD * rank), :]
    window[pl.ds(CHILD * rank, rank), :] = jnp.zeros((rank, bulk2.shape[1]), BF16)
    skip = CHILD * rank
    room = work.shape[1] // 2
    count = CHILD // 2
    stores = []
    for half in range(2):
        start = jnp.bitwise_xor(half, odd) * count
        for t in range(count):
            n = start + t
            picked = [window[blocks(work[7 + f, n], 1, rank), :] for f in range(FAR)]
            acc[blocks(n, 1, leaf), :] += mm(folded[n], jnp.concatenate(picked, axis=0))

        def step(t, _):
            for b in range(BATCH):
                n = half * room + t * BATCH + b
                for r, held, low in ((0, tiles, 0), (1, other, base)):
                    tile = work[3 * r, n]
                    at = pl.multiple_of(skip + work[3 * r + 1, n] * leaf, rank)
                    part = mm(held[low + tile // slots, lax.rem(tile, slots)], bulk2[pl.ds(at, leaf), :])
                    acc[blocks(work[3 * r + 2, n], 1, leaf), :] += part
            return 0

        lax.fori_loop(0, work[6, half], step, 0)
        stores.append(
            pltpu.make_async_copy(acc.at[blocks(start, count, leaf)], out.at[blocks(base + start, count, leaf)], sems.at[half])
        )
        stores[-1].start()
    for store in stores:
        store.wait()


def shards(
    sources,
    near_tiles,
    near_index,
    near_count,
    leaf_basis,
    leaf_coupling,
    leaf_far,
    up_leaf,
    mid_coupling,
    mid_far,
    up_mid,
    top_coupling,
):
    sds = jax.ShapeDtypeStruct
    leaves, rank, leaf = leaf_basis.shape
    mids = up_leaf.shape[0]
    cols = sources.shape[1]
    slots = near_tiles.shape[1]
    total_top = top_coupling.shape[0]
    devices = lax.axis_size("leaf")
    group = CHILD // mids
    edge = CHILD * leaf
    edge_c = CHILD * rank
    rows = leaves * leaf
    assert leaves == 2 * CHILD and group == 4 and total_top >= 4
    product_flops = 2 * leaf * leaf * cols

    rest = [(i, i + 1) for i in range(1, devices - 1, 2)]
    rest = rest + [(j, i) for i, j in rest]

    def swap(k):
        return [(i, i ^ k) for i in range(devices)]

    def send(x, pairs, axis="leaf"):
        return lax.ppermute(x, axis, pairs)

    def call(kernel, out_shape, in_specs, out_specs, scratch, mib, estimate, **more):
        def run(*args):
            return pl.pallas_call(
                kernel,
                out_shape=out_shape,
                in_specs=in_specs,
                out_specs=out_specs,
                scratch_shapes=scratch,
                compiler_params=params(mib),
                cost_estimate=estimate,
                **more,
            )(*args)

        return run

    index, count, far_index, mid_index = map(in_hbm, (near_index.T, near_count, leaf_far.T, mid_far))
    own_tiles = in_hbm(near_tiles)

    pack, bulk1, coef, src = call(
        upward,
        (
            sds(((mids + 1) * rank, cols), BF16),
            sds((edge_c + edge, cols), BF16),
            sds((leaves * rank, cols), BF16),
            sds((rows + leaf, cols), BF16),
        ),
        [HBM] * 4,
        (VMEM,) * 4,
        [
            pltpu.VMEM(leaf_basis.shape, BF16),
            pltpu.VMEM(up_leaf.shape, BF16),
            pltpu.VMEM(up_mid.shape, BF16),
            pltpu.SemaphoreType.DMA((2 * PARTS + 2,)),
        ],
        8,
        cost(2 * leaves * rank * leaf * cols, 4 << 20),
    )(*map(in_hbm, (sources, leaf_basis, up_leaf, up_mid)))
    src = in_vmem(src)

    pack1 = send(pack, swap(1))
    bulk1 = send(bulk1, swap(1))
    other = in_vmem(send(near_tiles, [(0, 1), (1, 0)], "col"))

    work, bulk2 = call(
        prepare,
        (sds((7 + FAR, CHILD * slots + 2 * BATCH), jnp.int32), sds((edge_c + edge, cols), BF16)),
        [SMEM, SMEM, SMEM, VMEM, VMEM],
        (SMEM, VMEM),
        [],
        8,
        cost(0, 4 << 20),
    )(index, count, far_index, coef, src)

    held = mids * rank
    pair, part = call(
        join,
        (sds((2 * held + rank, cols), BF16), sds((rank, cols), BF16)),
        [VMEM] * 2,
        (VMEM,) * 2,
        [],
        4,
        cost(0, 1 << 18),
    )(pack, pack1)

    pair1 = send(pair, swap(2))
    parts = [send(part, swap(k * group)) for k in range(2, total_top)]
    plane = call(
        cluster,
        sds((4 * held + rank, cols), BF16),
        [VMEM] * 2,
        VMEM,
        [],
        4,
        cost(0, 1 << 18),
    )(pair, pair1)
    beyond = call(
        stacked,
        sds(((total_top - 2) * rank, cols), BF16),
        [VMEM] * len(parts),
        VMEM,
        [],
        4,
        cost(0, 1 << 18),
    )(*parts)
    next_pairs = [(i, i + group) for i in range(group, devices - group) if i % (2 * group) >= group]
    next_a = send(plane, swap(group))
    next_b = send(plane, next_pairs + [(j, i) for i, j in next_pairs])
    beyond1 = send(beyond, swap(2))
    bulk2 = send(bulk2, rest)

    folded = None
    for late in (False, True):
        held = [] if folded is None else [in_vmem(folded)]
        folded = call(
            functools.partial(fold, late, devices - group),
            sds((CHILD, leaf, leaf_coupling.shape[2]), BF16),
            [HBM] * 2 + [VMEM] * len(held),
            VMEM,
            [
                pltpu.VMEM((CHILD,) + leaf_basis.shape[1:], BF16),
                pltpu.VMEM((CHILD,) + leaf_coupling.shape[1:], BF16),
                pltpu.SemaphoreType.DMA((2,)),
            ],
            6,
            cost(CHILD * 2 * leaf * leaf * rank, 2 << 20),
            **({"input_output_aliases": {2: 0}} if held else {}),
        )(in_hbm(leaf_basis), in_hbm(leaf_coupling), *held)

    half_tiles = (CHILD,) + near_tiles.shape[1:]
    near1, near2, tiles2 = call(
        near_most,
        (sds((edge, cols), F32), sds((edge, cols), F32), sds(half_tiles, BF16)),
        [SMEM, SMEM, HBM] + [VMEM] * 3,
        (VMEM,) * 3,
        [
            pltpu.VMEM(half_tiles, BF16),
            pltpu.VMEM((rows + edge + leaf, cols), BF16),
            pltpu.SemaphoreType.DMA((CHILD,)),
            pltpu.SemaphoreType.DMA((CHILD,)),
        ],
        20,
        cost(leaves * 2 * slots * product_flops, 16 << 20),
    )(index, count, own_tiles, other, src, bulk1)

    out, acc2 = call(
        downward,
        (sds((rows, cols), F32), sds((edge + leaf, cols), F32)),
        [SMEM] * 2 + [VMEM] * 15,
        (ANY, VMEM),
        [
            pltpu.VMEM((edge, cols), F32),
            pltpu.VMEM((leaves * rank, cols), F32),
            pltpu.VMEM((edge_c + (leaves + 1) * rank, cols), BF16),
            pltpu.VMEM((mids * FAR * rank, cols), BF16),
            pltpu.VMEM((total_top * rank, cols), BF16),
            pltpu.SemaphoreType.DMA((CHILD // 2,)),
        ],
        16,
        cost(leaves * 4 * product_flops, 12 << 20),
    )(
        far_index, mid_index,
        near1, near2, coef, bulk1, plane, next_a, next_b, beyond, beyond1,
        leaf_basis, leaf_coupling, up_leaf, mid_coupling, up_mid, top_coupling,
    )

    product, _ = call(
        near_last,
        (sds((rows, cols), F32), sds((edge + leaf, cols), F32)),
        [SMEM] + [VMEM] * 5 + [ANY],
        (ANY, VMEM),
        [pltpu.VMEM((edge_c + rank, cols), BF16), pltpu.SemaphoreType.DMA((2,))],
        8,
        cost(leaves * slots * product_flops, 4 << 20),
        input_output_aliases={6: 0, 4: 1},
    )(work, in_vmem(tiles2), other, bulk2, in_vmem(acc2), folded, out)
    return product


def solution(mesh):


    return jax.shard_map(
        shards,
        mesh=mesh,
        in_specs=(
            P("leaf", "col"),
            P("leaf", "col", None, None),
            P("leaf", None),
            P("leaf"),
            P("leaf", None, None),
            P("leaf", None, None),
            P("leaf", None),
            P("leaf", None, None),
            P("leaf", None, None),
            P("leaf", None),
            P("leaf", None, None),
            P(),
        ),
        out_specs=P("leaf", "col"),
        check_vma=False,
    )
```

```python
import functools

import jax
import jax.numpy as jnp
from jax import lax
from jax.experimental import pallas as pl
from jax.experimental.pallas import tpu as pltpu
from jax.sharding import PartitionSpec as P


CHILD = 8
FAR = 4
BATCH = 4
PARTS = 2

F32 = jnp.float32
BF16 = jnp.bfloat16
VMEM = pl.BlockSpec(memory_space=pltpu.VMEM)
SMEM = pl.BlockSpec(memory_space=pltpu.SMEM)
HBM = pl.BlockSpec(memory_space=pltpu.HBM)
ANY = pl.BlockSpec(memory_space=pl.ANY)


def mm(a, b):
    return jnp.dot(a, b, preferred_element_type=F32)


def mm_t(a, b):
    return lax.dot_general(a, b, (((0,), (0,)), ((), ())), preferred_element_type=F32)


def cost(flops, nbytes):
    return pl.CostEstimate(flops=flops, transcendentals=0, bytes_accessed=nbytes)


def params(mib):
    return pltpu.CompilerParams(vmem_limit_bytes=mib << 20)


def in_vmem(x):
    return pltpu.with_memory_space_constraint(x, pltpu.VMEM)


def in_hbm(x):
    return pltpu.with_memory_space_constraint(x, pltpu.HBM)


def blocks(start, count, size):
    return pl.ds(pl.multiple_of(start * size, size), count * size)


def upward(
    src_hbm, basis_hbm, up_leaf_hbm, up_mid_hbm,
    pack, bulk1, coef, src,
    basis, up_leaf, up_mid, sems,
):
    leaves, rank, leaf = basis.shape
    mids = up_leaf.shape[0]
    step = leaves // PARTS
    loads = []
    for p in range(PARTS):
        near = pl.ds(p * step * leaf, step * leaf)
        far = pl.ds(p * step, step)
        loads.append(pltpu.make_async_copy(src_hbm.at[near], src.at[near], sems.at[2 * p]))
        loads.append(pltpu.make_async_copy(basis_hbm.at[far], basis.at[far], sems.at[2 * p + 1]))
    loads.append(pltpu.make_async_copy(up_leaf_hbm, up_leaf, sems.at[2 * PARTS]))
    loads.append(pltpu.make_async_copy(up_mid_hbm, up_mid, sems.at[2 * PARTS + 1]))
    for load in loads:
        load.start()
    src[pl.ds(leaves * leaf, leaf), :] = jnp.zeros((leaf, src.shape[1]), BF16)
    odd = lax.rem(lax.axis_index("leaf"), 2)
    for p in range(PARTS):
        loads[2 * p].wait()
        loads[2 * p + 1].wait()
        for i in range(p * step, (p + 1) * step):
            coef[pl.ds(i * rank, rank), :] = mm(basis[i], src[pl.ds(i * leaf, leaf), :]).astype(BF16)
    first = (1 - odd) * (leaves - CHILD)
    bulk1[pl.ds(0, CHILD * rank), :] = coef[blocks(first, CHILD, rank), :]
    bulk1[pl.ds(CHILD * rank, CHILD * leaf), :] = src[blocks(first, CHILD, leaf), :]
    loads[2 * PARTS].wait()
    loads[2 * PARTS + 1].wait()
    total = None
    for q in range(mids):
        mid = mm(up_leaf[q], coef[pl.ds(q * CHILD * rank, CHILD * rank), :]).astype(BF16)
        pack[pl.ds(q * rank, rank), :] = mid
        lift = mm(up_mid[q], mid).astype(BF16).astype(F32)
        total = lift if total is None else total + lift
    pack[pl.ds(mids * rank, rank), :] = total.astype(BF16)


def prepare(index, count, leaf_far, coef, src, work, bulk2):
    leaves = index.shape[1]
    slots = index.shape[0] // 2
    rank = coef.shape[0] // leaves
    leaf = src.shape[0] // (leaves + 1)
    device = lax.axis_index("leaf")
    odd = lax.rem(device, 2)
    core = lax.axis_index("col")
    base = odd * (leaves - CHILD)
    bulk2[pl.ds(0, CHILD * rank), :] = coef[blocks(base, CHILD, rank), :]
    bulk2[pl.ds(CHILD * rank, CHILD * leaf), :] = src[blocks(base, CHILD, leaf), :]
    lowest = jnp.where(odd == 1, leaves, -CHILD) + device * leaves

    room = work.shape[1] // 2
    for part in range(2):
        start = jnp.bitwise_xor(part, odd) * (CHILD // 2)

        def row(t, found):
            n = start + t
            live = count[base + n]
            for f in range(FAR):
                at = leaf_far[f, base + n] - lowest
                work[7 + f, n] = jnp.where((at >= 0) & (at < CHILD), at, CHILD)
            out = []
            for r, owner in ((0, core), (1, 1 - core)):
                at = found[r]
                for k in range(slots):
                    slot = owner * slots + k
                    outside = index[slot, base + n] - lowest
                    work[3 * r, at] = n * slots + k
                    work[3 * r + 1, at] = outside
                    work[3 * r + 2, at] = n
                    use = (slot < live) & (outside >= 0) & (outside < CHILD)
                    at = at + use.astype(jnp.int32)
                out.append(at)
            return tuple(out)

        begin = jnp.int32(part * room)
        found = lax.fori_loop(0, CHILD // 2, row, (begin, begin))
        rounds = (jnp.maximum(found[0], found[1]) - begin + BATCH - 1) // BATCH
        work[6, part] = rounds
        for r in range(2):

            def fill(n, _):
                work[3 * r, n] = 0
                work[3 * r + 1, n] = 0
                work[3 * r + 2, n] = CHILD
                return 0

            lax.fori_loop(found[r], begin + rounds * BATCH, fill, 0)


def fold(group, after, basis_hbm, coupling_hbm, *refs):
    folded, basis, coupling, sems = refs[-4:]
    leaves, _, _ = basis_hbm.shape
    device = lax.axis_index("leaf")
    base = lax.rem(device, 2) * (leaves - CHILD)
    parent = device // group
    member = lax.rem(device, group)
    inner = (member > 0) & (member < group - 1)
    early = (parent >= 2) | ((parent == 1) & inner)

    @pl.when(early != after)
    def _():
        loads = [
            pltpu.make_async_copy(a.at[pl.ds(base, CHILD)], b, sems.at[k])
            for k, (a, b) in enumerate(((basis_hbm, basis), (coupling_hbm, coupling)))
        ]
        for load in loads:
            load.start()
        for load in loads:
            load.wait()
        for n in range(CHILD):
            folded[n] = mm_t(basis[n], coupling[n]).astype(BF16)


def join(pack, pack1, pair, part):
    held = part.shape[0]
    mids = pack.shape[0] - held
    total = pack[pl.ds(mids, held), :].astype(F32) + pack1[pl.ds(mids, held), :].astype(F32)
    pair[pl.ds(0, mids), :] = pack[pl.ds(0, mids), :]
    pair[pl.ds(mids, mids), :] = pack1[pl.ds(0, mids), :]
    pair[pl.ds(2 * mids, held), :] = total.astype(BF16)
    part[...] = total.astype(BF16)


def cluster(pair, pair1, plane):
    mids = plane.shape[0] - pair.shape[0]
    held = pair.shape[0] - mids
    plane[pl.ds(0, mids), :] = pair[pl.ds(0, mids), :]
    plane[pl.ds(mids, mids), :] = pair1[pl.ds(0, mids), :]
    total = pair[pl.ds(mids, held), :].astype(F32) + pair1[pl.ds(mids, held), :].astype(F32)
    plane[pl.ds(2 * mids, held), :] = total.astype(BF16)


def stacked(*refs):
    out = refs[-1]
    held = refs[0].shape[0]
    for k, part in enumerate(refs[:-1]):
        out[pl.ds(k * held, held), :] = part[...]


def load_tiles(tiles_hbm, tiles, sems, base):
    loads = [
        pltpu.make_async_copy(tiles_hbm.at[base + n], tiles.at[n], sems.at[n])
        for n in range(tiles.shape[0])
    ]
    for load in loads:
        load.start()
    return loads


def product(index, live, held, n, k, slot, i, window, lowest, total):
    leaf = held.shape[3]
    at = index[slot, i] - lowest
    place = jnp.where((slot < live) & (at >= 0) & (at < total), at, total)
    return mm(held[n, k], window[blocks(place, 1, leaf), :])


def near_most(index, count, tiles_hbm, other, src, bulk1, acc1, acc2, tiles2, tiles1, window, sems1, sems2):
    leaves, slots, leaf, _ = other.shape
    device = lax.axis_index("leaf")
    odd = lax.rem(device, 2)
    core = lax.axis_index("col")
    base1 = (1 - odd) * (leaves - CHILD)
    base2 = odd * (leaves - CHILD)
    loads2 = load_tiles(tiles_hbm, tiles2, sems2, base2)
    loads1 = load_tiles(tiles_hbm, tiles1, sems1, base1)
    total = leaves + CHILD
    window[blocks(odd * CHILD, leaves, leaf), :] = src[pl.ds(0, leaves * leaf), :]
    window[blocks((1 - odd) * leaves, CHILD, leaf), :] = bulk1[pl.ds(bulk1.shape[0] - CHILD * leaf, CHILD * leaf), :]
    window[pl.ds(total * leaf, leaf), :] = jnp.zeros((leaf, src.shape[1]), BF16)
    lowest = device * leaves - odd * CHILD

    def others2(n, _):
        i = base2 + n
        acc2[blocks(n, 1, leaf), :] = sum(
            product(index, count[i], other, i, k, (1 - core) * slots + k, i, src, device * leaves, leaves)
            for k in range(slots)
        )
        return 0

    lax.fori_loop(0, CHILD, others2, 0, unroll=4)
    for load in loads2:
        load.wait()

    def own2(n, _):
        i = base2 + n
        acc2[blocks(n, 1, leaf), :] += sum(
            product(index, count[i], tiles2, n, k, core * slots + k, i, src, device * leaves, leaves)
            for k in range(slots)
        )
        return 0

    lax.fori_loop(0, CHILD, own2, 0, unroll=4)
    for load in loads1:
        load.wait()

    def all1(n, _):
        i = base1 + n
        acc1[blocks(n, 1, leaf), :] = sum(
            product(index, count[i], held, at, k, owner * slots + k, i, window, lowest, total)
            for held, at, owner in ((tiles1, n, core), (other, i, 1 - core))
            for k in range(slots)
        )
        return 0

    lax.fori_loop(0, CHILD, all1, 0, unroll=2)


def downward(
    leaf_far, mid_far,
    near1, near2, coef, bulk1, plane, next_a, next_b, beyond0, beyond1,
    basis, leaf_coupling, up_leaf, mid_coupling, up_mid, top_coupling,
    out, acc2,
    full, down, window, chosen, stack, sems,
):
    total_top = top_coupling.shape[0]
    leaves, rank, leaf = basis.shape
    mids = up_leaf.shape[0]
    group = CHILD // mids
    device = lax.axis_index("leaf")
    odd = lax.rem(device, 2)
    parent = device // group
    member = lax.rem(device, group)

    stack[blocks(parent, 1, rank), :] = jnp.zeros((rank, full.shape[1]), BF16)
    stack[blocks(jnp.bitwise_xor(parent, 1), 1, rank), :] = next_a[pl.ds(CHILD * rank, rank), :]
    for p in range(2, total_top):
        rows = pl.ds((p - 2) * rank, rank)
        top = beyond0[rows, :].astype(F32) + beyond1[rows, :].astype(F32)
        stack[blocks(jnp.bitwise_xor(parent, p), 1, rank), :] = top.astype(BF16)
    top_field = mm(top_coupling[parent], stack[...]).astype(BF16)

    total = leaves + CHILD
    lowest = device * leaves - odd * CHILD
    window[blocks(odd * CHILD, leaves, rank), :] = coef[...]
    window[blocks((1 - odd) * leaves, CHILD, rank), :] = bulk1[pl.ds(0, CHILD * rank), :]
    window[pl.ds(total * rank, rank), :] = jnp.zeros((rank, full.shape[1]), BF16)

    for q in range(mids):
        for f in range(FAR):
            b = mid_far[q, f]
            above = b // CHILD
            inside = lax.rem(b, CHILD)
            place = jnp.bitwise_xor(inside // mids, member) * mids + lax.rem(inside, mids)
            row = blocks(place, 1, rank)
            to = pl.ds((q * FAR + f) * rank, rank)
            beside = jnp.bitwise_xor(parent, 1)

            @pl.when(above == parent)
            def _():
                chosen[to, :] = plane[row, :]

            @pl.when(above == beside)
            def _():
                chosen[to, :] = next_a[row, :]

            @pl.when((above != parent) & (above != beside))
            def _():
                chosen[to, :] = next_b[row, :]

    for q in range(mids):
        picked = chosen[pl.ds(q * FAR * rank, FAR * rank), :]
        mid_field = (mm(mid_coupling[q], picked) + mm_t(up_mid[q], top_field)).astype(BF16)
        down[pl.ds(q * CHILD * rank, CHILD * rank), :] = mm_t(up_leaf[q], mid_field)

    def field_of(i):
        field = far_sum(leaf_far, leaf_coupling, window, i, lowest, total)
        return (field + down[blocks(i, 1, rank), :]).astype(BF16)

    base1 = (1 - odd) * (leaves - CHILD)
    base2 = odd * (leaves - CHILD)
    stores = []
    for n in range(CHILD):
        rows = pl.ds(n * leaf, leaf)
        full[rows, :] = near1[rows, :] + mm_t(basis[base1 + n], field_of(base1 + n))
        if n % 2 == 1:
            rows = pl.ds((n - 1) * leaf, 2 * leaf)
            stores.append(
                pltpu.make_async_copy(full.at[rows], out.at[blocks(base1 + n - 1, 2, leaf)], sems.at[n // 2])
            )
            stores[-1].start()
    for n in range(CHILD):
        rows = pl.ds(n * leaf, leaf)
        acc2[rows, :] = near2[rows, :] + mm_t(basis[base2 + n], field_of(base2 + n))
    for store in stores:
        store.wait()


def far_sum(leaf_far, leaf_coupling, window, i, lowest, total):
    rank = leaf_coupling.shape[1]
    picked = []
    for f in range(FAR):
        at = leaf_far[f, i] - lowest
        place = jnp.where((at >= 0) & (at < total), at, total)
        picked.append(window[blocks(place, 1, rank), :])
    return mm(leaf_coupling[i], jnp.concatenate(picked, axis=0))


def near_last(work, tiles, other, bulk2, acc_in, folded, out_in, out, acc, window, sems):
    leaves, slots, leaf, _ = other.shape
    rank = window.shape[0] // (CHILD + 1)
    odd = lax.rem(lax.axis_index("leaf"), 2)
    base = odd * (leaves - CHILD)
    window[pl.ds(0, CHILD * rank), :] = bulk2[pl.ds(0, CHILD * rank), :]
    window[pl.ds(CHILD * rank, rank), :] = jnp.zeros((rank, bulk2.shape[1]), BF16)
    skip = CHILD * rank
    room = work.shape[1] // 2
    count = CHILD // 2
    stores = []
    for half in range(2):
        start = jnp.bitwise_xor(half, odd) * count
        for t in range(count):
            n = start + t
            picked = [window[blocks(work[7 + f, n], 1, rank), :] for f in range(FAR)]
            acc[blocks(n, 1, leaf), :] += mm(folded[n], jnp.concatenate(picked, axis=0))

        def step(t, _):
            for b in range(BATCH):
                n = half * room + t * BATCH + b
                for r, held, low in ((0, tiles, 0), (1, other, base)):
                    tile = work[3 * r, n]
                    at = pl.multiple_of(skip + work[3 * r + 1, n] * leaf, rank)
                    part = mm(held[low + tile // slots, lax.rem(tile, slots)], bulk2[pl.ds(at, leaf), :])
                    acc[blocks(work[3 * r + 2, n], 1, leaf), :] += part
            return 0

        lax.fori_loop(0, work[6, half], step, 0)
        stores.append(
            pltpu.make_async_copy(acc.at[blocks(start, count, leaf)], out.at[blocks(base + start, count, leaf)], sems.at[half])
        )
        stores[-1].start()
    for store in stores:
        store.wait()


def shards(
    sources,
    near_tiles,
    near_index,
    near_count,
    leaf_basis,
    leaf_coupling,
    leaf_far,
    up_leaf,
    mid_coupling,
    mid_far,
    up_mid,
    top_coupling,
):
    sds = jax.ShapeDtypeStruct
    leaves, rank, leaf = leaf_basis.shape
    mids = up_leaf.shape[0]
    cols = sources.shape[1]
    slots = near_tiles.shape[1]
    total_top = top_coupling.shape[0]
    devices = lax.axis_size("leaf")
    group = CHILD // mids
    edge = CHILD * leaf
    edge_c = CHILD * rank
    rows = leaves * leaf
    assert leaves == 2 * CHILD and group == 4 and total_top >= 4
    product_flops = 2 * leaf * leaf * cols

    rest = [(i, i + 1) for i in range(1, devices - 1, 2)]
    rest = rest + [(j, i) for i, j in rest]

    def swap(k):
        return [(i, i ^ k) for i in range(devices)]

    def send(x, pairs, axis="leaf"):
        return lax.ppermute(x, axis, pairs)

    def call(kernel, out_shape, in_specs, out_specs, scratch, mib, estimate, **more):
        def run(*args):
            return pl.pallas_call(
                kernel,
                out_shape=out_shape,
                in_specs=in_specs,
                out_specs=out_specs,
                scratch_shapes=scratch,
                compiler_params=params(mib),
                cost_estimate=estimate,
                **more,
            )(*args)

        return run

    index, count, far_index, mid_index = map(in_hbm, (near_index.T, near_count, leaf_far.T, mid_far))
    own_tiles = in_hbm(near_tiles)

    pack, bulk1, coef, src = call(
        upward,
        (
            sds(((mids + 1) * rank, cols), BF16),
            sds((edge_c + edge, cols), BF16),
            sds((leaves * rank, cols), BF16),
            sds((rows + leaf, cols), BF16),
        ),
        [HBM] * 4,
        (VMEM,) * 4,
        [
            pltpu.VMEM(leaf_basis.shape, BF16),
            pltpu.VMEM(up_leaf.shape, BF16),
            pltpu.VMEM(up_mid.shape, BF16),
            pltpu.SemaphoreType.DMA((2 * PARTS + 2,)),
        ],
        8,
        cost(2 * leaves * rank * leaf * cols, 4 << 20),
    )(*map(in_hbm, (sources, leaf_basis, up_leaf, up_mid)))
    src = in_vmem(src)

    pack1 = send(pack, swap(1))
    bulk1 = send(bulk1, swap(1))
    other = in_vmem(send(near_tiles, [(0, 1), (1, 0)], "col"))

    work, bulk2 = call(
        prepare,
        (sds((7 + FAR, CHILD * slots + 2 * BATCH), jnp.int32), sds((edge_c + edge, cols), BF16)),
        [SMEM, SMEM, SMEM, VMEM, VMEM],
        (SMEM, VMEM),
        [],
        8,
        cost(0, 4 << 20),
    )(index, count, far_index, coef, src)

    held = mids * rank
    pair, part = call(
        join,
        (sds((2 * held + rank, cols), BF16), sds((rank, cols), BF16)),
        [VMEM] * 2,
        (VMEM,) * 2,
        [],
        4,
        cost(0, 1 << 18),
    )(pack, pack1)

    pair1 = send(pair, swap(2))
    parts = [send(part, swap(k * group)) for k in range(2, total_top)]
    plane = call(
        cluster,
        sds((4 * held + rank, cols), BF16),
        [VMEM] * 2,
        VMEM,
        [],
        4,
        cost(0, 1 << 18),
    )(pair, pair1)
    beyond = call(
        stacked,
        sds(((total_top - 2) * rank, cols), BF16),
        [VMEM] * len(parts),
        VMEM,
        [],
        4,
        cost(0, 1 << 18),
    )(*parts)
    next_pairs = [(i, i + group) for i in range(group, devices - group) if i % (2 * group) >= group]
    next_a = send(plane, swap(group))
    next_b = send(plane, next_pairs + [(j, i) for i, j in next_pairs])
    beyond1 = send(beyond, swap(2))
    bulk2 = send(bulk2, rest)

    folded = None
    for after in (False, True):
        held = [] if folded is None else [in_vmem(folded)]
        folded = call(
            functools.partial(fold, group, after),
            sds((CHILD, leaf, leaf_coupling.shape[2]), BF16),
            [HBM] * 2 + [VMEM] * len(held),
            VMEM,
            [
                pltpu.VMEM((CHILD,) + leaf_basis.shape[1:], BF16),
                pltpu.VMEM((CHILD,) + leaf_coupling.shape[1:], BF16),
                pltpu.SemaphoreType.DMA((2,)),
            ],
            6,
            cost(CHILD * 2 * leaf * leaf * rank, 2 << 20),
            **({"input_output_aliases": {2: 0}} if held else {}),
        )(in_hbm(leaf_basis), in_hbm(leaf_coupling), *held)

    half_tiles = (CHILD,) + near_tiles.shape[1:]
    near1, near2, tiles2 = call(
        near_most,
        (sds((edge, cols), F32), sds((edge, cols), F32), sds(half_tiles, BF16)),
        [SMEM, SMEM, HBM] + [VMEM] * 3,
        (VMEM,) * 3,
        [
            pltpu.VMEM(half_tiles, BF16),
            pltpu.VMEM((rows + edge + leaf, cols), BF16),
            pltpu.SemaphoreType.DMA((CHILD,)),
            pltpu.SemaphoreType.DMA((CHILD,)),
        ],
        20,
        cost(leaves * 2 * slots * product_flops, 16 << 20),
    )(index, count, own_tiles, other, src, bulk1)

    out, acc2 = call(
        downward,
        (sds((rows, cols), F32), sds((edge + leaf, cols), F32)),
        [SMEM] * 2 + [VMEM] * 15,
        (ANY, VMEM),
        [
            pltpu.VMEM((edge, cols), F32),
            pltpu.VMEM((leaves * rank, cols), F32),
            pltpu.VMEM((edge_c + (leaves + 1) * rank, cols), BF16),
            pltpu.VMEM((mids * FAR * rank, cols), BF16),
            pltpu.VMEM((total_top * rank, cols), BF16),
            pltpu.SemaphoreType.DMA((CHILD // 2,)),
        ],
        16,
        cost(leaves * 4 * product_flops, 12 << 20),
    )(
        far_index, mid_index,
        near1, near2, coef, bulk1, plane, next_a, next_b, beyond, beyond1,
        leaf_basis, leaf_coupling, up_leaf, mid_coupling, up_mid, top_coupling,
    )

    product, _ = call(
        near_last,
        (sds((rows, cols), F32), sds((edge + leaf, cols), F32)),
        [SMEM] + [VMEM] * 5 + [ANY],
        (ANY, VMEM),
        [pltpu.VMEM((edge_c + rank, cols), BF16), pltpu.SemaphoreType.DMA((2,))],
        8,
        cost(leaves * slots * product_flops, 4 << 20),
        input_output_aliases={6: 0, 4: 1},
    )(work, in_vmem(tiles2), other, bulk2, in_vmem(acc2), folded, out)
    return product


def solution(mesh):


    return jax.shard_map(
        shards,
        mesh=mesh,
        in_specs=(
            P("leaf", "col"),
            P("leaf", "col", None, None),
            P("leaf", None),
            P("leaf"),
            P("leaf", None, None),
            P("leaf", None, None),
            P("leaf", None),
            P("leaf", None, None),
            P("leaf", None, None),
            P("leaf", None),
            P("leaf", None, None),
            P(),
        ),
        out_specs=P("leaf", "col"),
        check_vma=False,
    )
```

```python
import functools

import jax
import jax.numpy as jnp
from jax import lax
from jax.experimental import pallas as pl
from jax.experimental.pallas import tpu as pltpu
from jax.sharding import PartitionSpec as P


CHILD = 8
FAR = 4
BATCH = 4
PARTS = 2

F32 = jnp.float32
BF16 = jnp.bfloat16
VMEM = pl.BlockSpec(memory_space=pltpu.VMEM)
SMEM = pl.BlockSpec(memory_space=pltpu.SMEM)
HBM = pl.BlockSpec(memory_space=pltpu.HBM)
ANY = pl.BlockSpec(memory_space=pl.ANY)


def mm(a, b):
    return jnp.dot(a, b, preferred_element_type=F32)


def mm_t(a, b):
    return lax.dot_general(a, b, (((0,), (0,)), ((), ())), preferred_element_type=F32)


def cost(flops, nbytes):
    return pl.CostEstimate(flops=flops, transcendentals=0, bytes_accessed=nbytes)


def params(mib):
    return pltpu.CompilerParams(vmem_limit_bytes=mib << 20)


def in_vmem(x):
    return pltpu.with_memory_space_constraint(x, pltpu.VMEM)


def in_hbm(x):
    return pltpu.with_memory_space_constraint(x, pltpu.HBM)


def blocks(start, count, size):
    return pl.ds(pl.multiple_of(start * size, size), count * size)


def upward(
    src_hbm, basis_hbm, up_leaf_hbm, up_mid_hbm,
    pack, bulk1, coef, src,
    basis, up_leaf, up_mid, sems,
):
    leaves, rank, leaf = basis.shape
    mids = up_leaf.shape[0]
    step = leaves // PARTS
    loads = []
    for p in range(PARTS):
        near = pl.ds(p * step * leaf, step * leaf)
        far = pl.ds(p * step, step)
        loads.append(pltpu.make_async_copy(src_hbm.at[near], src.at[near], sems.at[2 * p]))
        loads.append(pltpu.make_async_copy(basis_hbm.at[far], basis.at[far], sems.at[2 * p + 1]))
    loads.append(pltpu.make_async_copy(up_leaf_hbm, up_leaf, sems.at[2 * PARTS]))
    loads.append(pltpu.make_async_copy(up_mid_hbm, up_mid, sems.at[2 * PARTS + 1]))
    for load in loads:
        load.start()
    src[pl.ds(leaves * leaf, leaf), :] = jnp.zeros((leaf, src.shape[1]), BF16)
    odd = lax.rem(lax.axis_index("leaf"), 2)
    for p in range(PARTS):
        loads[2 * p].wait()
        loads[2 * p + 1].wait()
        for i in range(p * step, (p + 1) * step):
            coef[pl.ds(i * rank, rank), :] = mm(basis[i], src[pl.ds(i * leaf, leaf), :]).astype(BF16)
    first = (1 - odd) * (leaves - CHILD)
    bulk1[pl.ds(0, CHILD * rank), :] = coef[blocks(first, CHILD, rank), :]
    bulk1[pl.ds(CHILD * rank, CHILD * leaf), :] = src[blocks(first, CHILD, leaf), :]
    loads[2 * PARTS].wait()
    loads[2 * PARTS + 1].wait()
    total = None
    for q in range(mids):
        mid = mm(up_leaf[q], coef[pl.ds(q * CHILD * rank, CHILD * rank), :]).astype(BF16)
        pack[pl.ds(q * rank, rank), :] = mid
        lift = mm(up_mid[q], mid).astype(BF16).astype(F32)
        total = lift if total is None else total + lift
    pack[pl.ds(mids * rank, rank), :] = total.astype(BF16)


def prepare(index, count, leaf_far, coef, src, work, bulk2):
    leaves = index.shape[1]
    slots = index.shape[0] // 2
    rank = coef.shape[0] // leaves
    leaf = src.shape[0] // (leaves + 1)
    device = lax.axis_index("leaf")
    odd = lax.rem(device, 2)
    core = lax.axis_index("col")
    base = odd * (leaves - CHILD)
    bulk2[pl.ds(0, CHILD * rank), :] = coef[blocks(base, CHILD, rank), :]
    bulk2[pl.ds(CHILD * rank, CHILD * leaf), :] = src[blocks(base, CHILD, leaf), :]
    lowest = jnp.where(odd == 1, leaves, -CHILD) + device * leaves


    def row(n, found):
        live = count[base + n]
        for f in range(FAR):
            at = leaf_far[f, base + n] - lowest
            work[7 + f, n] = jnp.where((at >= 0) & (at < CHILD), at, CHILD)
        out = []
        for r, owner in ((0, core), (1, 1 - core)):
            at = found[r]
            for k in range(slots):
                slot = owner * slots + k
                outside = index[slot, base + n] - lowest
                work[3 * r, at] = n * slots + k
                work[3 * r + 1, at] = outside
                work[3 * r + 2, at] = n
                use = (slot < live) & (outside >= 0) & (outside < CHILD)
                at = at + use.astype(jnp.int32)
            out.append(at)
        return tuple(out)

    found = lax.fori_loop(0, CHILD, row, (jnp.int32(0), jnp.int32(0)))
    rounds = (jnp.maximum(found[0], found[1]) + BATCH - 1) // BATCH
    work[6, 0] = rounds
    for r in range(2):

        def fill(n, _):
            work[3 * r, n] = 0
            work[3 * r + 1, n] = 0
            work[3 * r + 2, n] = CHILD
            return 0

        lax.fori_loop(found[r], rounds * BATCH, fill, 0)


def fold(group, after, basis_hbm, coupling_hbm, *refs):
    folded, basis, coupling, sems = refs[-4:]
    leaves, _, _ = basis_hbm.shape
    device = lax.axis_index("leaf")
    base = lax.rem(device, 2) * (leaves - CHILD)
    parent = device // group
    member = lax.rem(device, group)
    inner = (member > 0) & (member < group - 1)
    early = (parent >= 2) | ((parent == 1) & inner)

    @pl.when(early != after)
    def _():
        loads = [
            pltpu.make_async_copy(a.at[pl.ds(base, CHILD)], b, sems.at[k])
            for k, (a, b) in enumerate(((basis_hbm, basis), (coupling_hbm, coupling)))
        ]
        for load in loads:
            load.start()
        for load in loads:
            load.wait()
        for n in range(CHILD):
            folded[n] = mm_t(basis[n], coupling[n]).astype(BF16)


def join(pack, pack1, pair, part):
    held = part.shape[0]
    mids = pack.shape[0] - held
    total = pack[pl.ds(mids, held), :].astype(F32) + pack1[pl.ds(mids, held), :].astype(F32)
    pair[pl.ds(0, mids), :] = pack[pl.ds(0, mids), :]
    pair[pl.ds(mids, mids), :] = pack1[pl.ds(0, mids), :]
    pair[pl.ds(2 * mids, held), :] = total.astype(BF16)
    part[...] = total.astype(BF16)


def cluster(pair, pair1, plane):
    mids = plane.shape[0] - pair.shape[0]
    held = pair.shape[0] - mids
    plane[pl.ds(0, mids), :] = pair[pl.ds(0, mids), :]
    plane[pl.ds(mids, mids), :] = pair1[pl.ds(0, mids), :]
    total = pair[pl.ds(mids, held), :].astype(F32) + pair1[pl.ds(mids, held), :].astype(F32)
    plane[pl.ds(2 * mids, held), :] = total.astype(BF16)


def stacked(*refs):
    out = refs[-1]
    held = refs[0].shape[0]
    for k, part in enumerate(refs[:-1]):
        out[pl.ds(k * held, held), :] = part[...]


def load_tiles(tiles_hbm, tiles, sems, base):
    loads = [
        pltpu.make_async_copy(tiles_hbm.at[base + n], tiles.at[n], sems.at[n])
        for n in range(tiles.shape[0])
    ]
    for load in loads:
        load.start()
    return loads


def product(index, live, held, n, k, slot, i, window, lowest, total):
    leaf = held.shape[3]
    at = index[slot, i] - lowest
    place = jnp.where((slot < live) & (at >= 0) & (at < total), at, total)
    return mm(held[n, k], window[blocks(place, 1, leaf), :])


def near_most(index, count, tiles_hbm, other, src, bulk1, acc1, acc2, tiles2, tiles1, window, sems1, sems2):
    leaves, slots, leaf, _ = other.shape
    device = lax.axis_index("leaf")
    odd = lax.rem(device, 2)
    core = lax.axis_index("col")
    base1 = (1 - odd) * (leaves - CHILD)
    base2 = odd * (leaves - CHILD)
    loads2 = load_tiles(tiles_hbm, tiles2, sems2, base2)
    loads1 = load_tiles(tiles_hbm, tiles1, sems1, base1)
    total = leaves + CHILD
    window[blocks(odd * CHILD, leaves, leaf), :] = src[pl.ds(0, leaves * leaf), :]
    window[blocks((1 - odd) * leaves, CHILD, leaf), :] = bulk1[pl.ds(bulk1.shape[0] - CHILD * leaf, CHILD * leaf), :]
    window[pl.ds(total * leaf, leaf), :] = jnp.zeros((leaf, src.shape[1]), BF16)
    lowest = device * leaves - odd * CHILD

    def others2(n, _):
        i = base2 + n
        acc2[blocks(n, 1, leaf), :] = sum(
            product(index, count[i], other, i, k, (1 - core) * slots + k, i, src, device * leaves, leaves)
            for k in range(slots)
        )
        return 0

    lax.fori_loop(0, CHILD, others2, 0, unroll=4)
    for load in loads2:
        load.wait()

    def own2(n, _):
        i = base2 + n
        acc2[blocks(n, 1, leaf), :] += sum(
            product(index, count[i], tiles2, n, k, core * slots + k, i, src, device * leaves, leaves)
            for k in range(slots)
        )
        return 0

    lax.fori_loop(0, CHILD, own2, 0, unroll=4)
    for load in loads1:
        load.wait()

    def all1(n, _):
        i = base1 + n
        acc1[blocks(n, 1, leaf), :] = sum(
            product(index, count[i], held, at, k, owner * slots + k, i, window, lowest, total)
            for held, at, owner in ((tiles1, n, core), (other, i, 1 - core))
            for k in range(slots)
        )
        return 0

    lax.fori_loop(0, CHILD, all1, 0, unroll=2)


def downward(
    leaf_far, mid_far,
    near1, near2, coef, bulk1, plane, next_a, next_b, beyond0, beyond1,
    basis, leaf_coupling, up_leaf, mid_coupling, up_mid, top_coupling,
    out, acc2,
    full, down, window, chosen, stack, sems,
):
    total_top = top_coupling.shape[0]
    leaves, rank, leaf = basis.shape
    mids = up_leaf.shape[0]
    group = CHILD // mids
    device = lax.axis_index("leaf")
    odd = lax.rem(device, 2)
    parent = device // group
    member = lax.rem(device, group)

    stack[blocks(parent, 1, rank), :] = jnp.zeros((rank, full.shape[1]), BF16)
    stack[blocks(jnp.bitwise_xor(parent, 1), 1, rank), :] = next_a[pl.ds(CHILD * rank, rank), :]
    for p in range(2, total_top):
        rows = pl.ds((p - 2) * rank, rank)
        top = beyond0[rows, :].astype(F32) + beyond1[rows, :].astype(F32)
        stack[blocks(jnp.bitwise_xor(parent, p), 1, rank), :] = top.astype(BF16)
    top_field = mm(top_coupling[parent], stack[...]).astype(BF16)

    total = leaves + CHILD
    lowest = device * leaves - odd * CHILD
    window[blocks(odd * CHILD, leaves, rank), :] = coef[...]
    window[blocks((1 - odd) * leaves, CHILD, rank), :] = bulk1[pl.ds(0, CHILD * rank), :]
    window[pl.ds(total * rank, rank), :] = jnp.zeros((rank, full.shape[1]), BF16)

    for q in range(mids):
        for f in range(FAR):
            b = mid_far[q, f]
            above = b // CHILD
            inside = lax.rem(b, CHILD)
            place = jnp.bitwise_xor(inside // mids, member) * mids + lax.rem(inside, mids)
            row = blocks(place, 1, rank)
            to = pl.ds((q * FAR + f) * rank, rank)
            beside = jnp.bitwise_xor(parent, 1)

            @pl.when(above == parent)
            def _():
                chosen[to, :] = plane[row, :]

            @pl.when(above == beside)
            def _():
                chosen[to, :] = next_a[row, :]

            @pl.when((above != parent) & (above != beside))
            def _():
                chosen[to, :] = next_b[row, :]

    for q in range(mids):
        picked = chosen[pl.ds(q * FAR * rank, FAR * rank), :]
        mid_field = (mm(mid_coupling[q], picked) + mm_t(up_mid[q], top_field)).astype(BF16)
        down[pl.ds(q * CHILD * rank, CHILD * rank), :] = mm_t(up_leaf[q], mid_field)

    def field_of(i):
        field = far_sum(leaf_far, leaf_coupling, window, i, lowest, total)
        return (field + down[blocks(i, 1, rank), :]).astype(BF16)

    base1 = (1 - odd) * (leaves - CHILD)
    base2 = odd * (leaves - CHILD)
    stores = []
    for n in range(CHILD):
        rows = pl.ds(n * leaf, leaf)
        full[rows, :] = near1[rows, :] + mm_t(basis[base1 + n], field_of(base1 + n))
        if n % 2 == 1:
            rows = pl.ds((n - 1) * leaf, 2 * leaf)
            stores.append(
                pltpu.make_async_copy(full.at[rows], out.at[blocks(base1 + n - 1, 2, leaf)], sems.at[n // 2])
            )
            stores[-1].start()
    for n in range(CHILD):
        rows = pl.ds(n * leaf, leaf)
        acc2[rows, :] = near2[rows, :] + mm_t(basis[base2 + n], field_of(base2 + n))
    for store in stores:
        store.wait()


def far_sum(leaf_far, leaf_coupling, window, i, lowest, total):
    rank = leaf_coupling.shape[1]
    picked = []
    for f in range(FAR):
        at = leaf_far[f, i] - lowest
        place = jnp.where((at >= 0) & (at < total), at, total)
        picked.append(window[blocks(place, 1, rank), :])
    return mm(leaf_coupling[i], jnp.concatenate(picked, axis=0))


def near_last(work, tiles, other, bulk2, acc_in, folded, out_in, out, acc, window, sems):
    leaves, slots, leaf, _ = other.shape
    rank = window.shape[0] // (CHILD + 1)
    odd = lax.rem(lax.axis_index("leaf"), 2)
    base = odd * (leaves - CHILD)
    window[pl.ds(0, CHILD * rank), :] = bulk2[pl.ds(0, CHILD * rank), :]
    window[pl.ds(CHILD * rank, rank), :] = jnp.zeros((rank, bulk2.shape[1]), BF16)
    skip = CHILD * rank

    def step(t, _):
        for b in range(BATCH):
            n = t * BATCH + b
            for r, held, low in ((0, tiles, 0), (1, other, base)):
                tile = work[3 * r, n]
                at = pl.multiple_of(skip + work[3 * r + 1, n] * leaf, rank)
                part = mm(held[low + tile // slots, lax.rem(tile, slots)], bulk2[pl.ds(at, leaf), :])
                acc[blocks(work[3 * r + 2, n], 1, leaf), :] += part
        return 0

    lax.fori_loop(0, work[6, 0], step, 0)
    stores = []
    for n in range(CHILD):
        rows = pl.ds(n * leaf, leaf)
        picked = [window[blocks(work[7 + f, n], 1, rank), :] for f in range(FAR)]
        acc[rows, :] += mm(folded[n], jnp.concatenate(picked, axis=0))
        stores.append(pltpu.make_async_copy(acc.at[rows], out.at[blocks(base + n, 1, leaf)], sems.at[n]))
        stores[-1].start()
    for store in stores:
        store.wait()


def shards(
    sources,
    near_tiles,
    near_index,
    near_count,
    leaf_basis,
    leaf_coupling,
    leaf_far,
    up_leaf,
    mid_coupling,
    mid_far,
    up_mid,
    top_coupling,
):
    sds = jax.ShapeDtypeStruct
    leaves, rank, leaf = leaf_basis.shape
    mids = up_leaf.shape[0]
    cols = sources.shape[1]
    slots = near_tiles.shape[1]
    total_top = top_coupling.shape[0]
    devices = lax.axis_size("leaf")
    group = CHILD // mids
    edge = CHILD * leaf
    edge_c = CHILD * rank
    rows = leaves * leaf
    assert leaves == 2 * CHILD and group == 4 and total_top >= 4
    product_flops = 2 * leaf * leaf * cols

    rest = [(i, i + 1) for i in range(1, devices - 1, 2)]
    rest = rest + [(j, i) for i, j in rest]

    def swap(k):
        return [(i, i ^ k) for i in range(devices)]

    def send(x, pairs, axis="leaf"):
        return lax.ppermute(x, axis, pairs)

    def call(kernel, out_shape, in_specs, out_specs, scratch, mib, estimate, **more):
        def run(*args):
            return pl.pallas_call(
                kernel,
                out_shape=out_shape,
                in_specs=in_specs,
                out_specs=out_specs,
                scratch_shapes=scratch,
                compiler_params=params(mib),
                cost_estimate=estimate,
                **more,
            )(*args)

        return run

    index, count, far_index, mid_index = map(in_hbm, (near_index.T, near_count, leaf_far.T, mid_far))
    own_tiles = in_hbm(near_tiles)

    pack, bulk1, coef, src = call(
        upward,
        (
            sds(((mids + 1) * rank, cols), BF16),
            sds((edge_c + edge, cols), BF16),
            sds((leaves * rank, cols), BF16),
            sds((rows + leaf, cols), BF16),
        ),
        [HBM] * 4,
        (VMEM,) * 4,
        [
            pltpu.VMEM(leaf_basis.shape, BF16),
            pltpu.VMEM(up_leaf.shape, BF16),
            pltpu.VMEM(up_mid.shape, BF16),
            pltpu.SemaphoreType.DMA((2 * PARTS + 2,)),
        ],
        8,
        cost(2 * leaves * rank * leaf * cols, 4 << 20),
    )(*map(in_hbm, (sources, leaf_basis, up_leaf, up_mid)))
    src = in_vmem(src)

    pack1 = send(pack, swap(1))
    bulk1 = send(bulk1, swap(1))
    other = in_vmem(send(near_tiles, [(0, 1), (1, 0)], "col"))

    work, bulk2 = call(
        prepare,
        (sds((7 + FAR, CHILD * slots + BATCH), jnp.int32), sds((edge_c + edge, cols), BF16)),
        [SMEM, SMEM, SMEM, VMEM, VMEM],
        (SMEM, VMEM),
        [],
        8,
        cost(0, 4 << 20),
    )(index, count, far_index, coef, src)

    held = mids * rank
    pair, part = call(
        join,
        (sds((2 * held + rank, cols), BF16), sds((rank, cols), BF16)),
        [VMEM] * 2,
        (VMEM,) * 2,
        [],
        4,
        cost(0, 1 << 18),
    )(pack, pack1)

    pair1 = send(pair, swap(2))
    parts = [send(part, swap(k * group)) for k in range(2, total_top)]
    plane = call(
        cluster,
        sds((4 * held + rank, cols), BF16),
        [VMEM] * 2,
        VMEM,
        [],
        4,
        cost(0, 1 << 18),
    )(pair, pair1)
    beyond = call(
        stacked,
        sds(((total_top - 2) * rank, cols), BF16),
        [VMEM] * len(parts),
        VMEM,
        [],
        4,
        cost(0, 1 << 18),
    )(*parts)
    next_pairs = [(i, i + group) for i in range(group, devices - group) if i % (2 * group) >= group]
    next_a = send(plane, swap(group))
    next_b = send(plane, next_pairs + [(j, i) for i, j in next_pairs])
    beyond1 = send(beyond, swap(2))
    bulk2 = send(bulk2, rest)

    folded = None
    for after in (False, True):
        held = [] if folded is None else [in_vmem(folded)]
        folded = call(
            functools.partial(fold, group, after),
            sds((CHILD, leaf, leaf_coupling.shape[2]), BF16),
            [HBM] * 2 + [VMEM] * len(held),
            VMEM,
            [
                pltpu.VMEM((CHILD,) + leaf_basis.shape[1:], BF16),
                pltpu.VMEM((CHILD,) + leaf_coupling.shape[1:], BF16),
                pltpu.SemaphoreType.DMA((2,)),
            ],
            6,
            cost(CHILD * 2 * leaf * leaf * rank, 2 << 20),
            **({"input_output_aliases": {2: 0}} if held else {}),
        )(in_hbm(leaf_basis), in_hbm(leaf_coupling), *held)

    half_tiles = (CHILD,) + near_tiles.shape[1:]
    near1, near2, tiles2 = call(
        near_most,
        (sds((edge, cols), F32), sds((edge, cols), F32), sds(half_tiles, BF16)),
        [SMEM, SMEM, HBM] + [VMEM] * 3,
        (VMEM,) * 3,
        [
            pltpu.VMEM(half_tiles, BF16),
            pltpu.VMEM((rows + edge + leaf, cols), BF16),
            pltpu.SemaphoreType.DMA((CHILD,)),
            pltpu.SemaphoreType.DMA((CHILD,)),
        ],
        20,
        cost(leaves * 2 * slots * product_flops, 16 << 20),
    )(index, count, own_tiles, other, src, bulk1)

    out, acc2 = call(
        downward,
        (sds((rows, cols), F32), sds((edge + leaf, cols), F32)),
        [SMEM] * 2 + [VMEM] * 15,
        (ANY, VMEM),
        [
            pltpu.VMEM((edge, cols), F32),
            pltpu.VMEM((leaves * rank, cols), F32),
            pltpu.VMEM((edge_c + (leaves + 1) * rank, cols), BF16),
            pltpu.VMEM((mids * FAR * rank, cols), BF16),
            pltpu.VMEM((total_top * rank, cols), BF16),
            pltpu.SemaphoreType.DMA((CHILD // 2,)),
        ],
        16,
        cost(leaves * 4 * product_flops, 12 << 20),
    )(
        far_index, mid_index,
        near1, near2, coef, bulk1, plane, next_a, next_b, beyond, beyond1,
        leaf_basis, leaf_coupling, up_leaf, mid_coupling, up_mid, top_coupling,
    )

    product, _ = call(
        near_last,
        (sds((rows, cols), F32), sds((edge + leaf, cols), F32)),
        [SMEM] + [VMEM] * 5 + [ANY],
        (ANY, VMEM),
        [pltpu.VMEM((edge_c + rank, cols), BF16), pltpu.SemaphoreType.DMA((CHILD,))],
        8,
        cost(leaves * slots * product_flops, 4 << 20),
        input_output_aliases={6: 0, 4: 1},
    )(work, in_vmem(tiles2), other, bulk2, in_vmem(acc2), folded, out)
    return product


def solution(mesh):


    return jax.shard_map(
        shards,
        mesh=mesh,
        in_specs=(
            P("leaf", "col"),
            P("leaf", "col", None, None),
            P("leaf", None),
            P("leaf"),
            P("leaf", None, None),
            P("leaf", None, None),
            P("leaf", None),
            P("leaf", None, None),
            P("leaf", None, None),
            P("leaf", None),
            P("leaf", None, None),
            P(),
        ),
        out_specs=P("leaf", "col"),
        check_vma=False,
    )
```

```python
import functools

import jax
import jax.numpy as jnp
from jax import lax
from jax.experimental import pallas as pl
from jax.experimental.pallas import tpu as pltpu
from jax.sharding import PartitionSpec as P


CHILD = 8
FAR = 4
BATCH = 4
PARTS = 2

F32 = jnp.float32
BF16 = jnp.bfloat16
VMEM = pl.BlockSpec(memory_space=pltpu.VMEM)
SMEM = pl.BlockSpec(memory_space=pltpu.SMEM)
HBM = pl.BlockSpec(memory_space=pltpu.HBM)
ANY = pl.BlockSpec(memory_space=pl.ANY)


def mm(a, b):
    return jnp.dot(a, b, preferred_element_type=F32)


def mm_t(a, b):
    return lax.dot_general(a, b, (((0,), (0,)), ((), ())), preferred_element_type=F32)


def cost(flops, nbytes):
    return pl.CostEstimate(flops=flops, transcendentals=0, bytes_accessed=nbytes)


def params(mib):
    return pltpu.CompilerParams(vmem_limit_bytes=mib << 20)


def in_vmem(x):
    return pltpu.with_memory_space_constraint(x, pltpu.VMEM)


def in_hbm(x):
    return pltpu.with_memory_space_constraint(x, pltpu.HBM)


def blocks(start, count, size):
    return pl.ds(pl.multiple_of(start * size, size), count * size)


def upward(
    src_hbm, basis_hbm, up_leaf_hbm, up_mid_hbm,
    pack, bulk1, coef, src,
    basis, up_leaf, up_mid, sems,
):
    leaves, rank, leaf = basis.shape
    mids = up_leaf.shape[0]
    step = leaves // PARTS
    loads = []
    for p in range(PARTS):
        near = pl.ds(p * step * leaf, step * leaf)
        far = pl.ds(p * step, step)
        loads.append(pltpu.make_async_copy(src_hbm.at[near], src.at[near], sems.at[2 * p]))
        loads.append(pltpu.make_async_copy(basis_hbm.at[far], basis.at[far], sems.at[2 * p + 1]))
    loads.append(pltpu.make_async_copy(up_leaf_hbm, up_leaf, sems.at[2 * PARTS]))
    loads.append(pltpu.make_async_copy(up_mid_hbm, up_mid, sems.at[2 * PARTS + 1]))
    for load in loads:
        load.start()
    src[pl.ds(leaves * leaf, leaf), :] = jnp.zeros((leaf, src.shape[1]), BF16)
    odd = lax.rem(lax.axis_index("leaf"), 2)
    for p in range(PARTS):
        loads[2 * p].wait()
        loads[2 * p + 1].wait()
        for i in range(p * step, (p + 1) * step):
            coef[pl.ds(i * rank, rank), :] = mm(basis[i], src[pl.ds(i * leaf, leaf), :]).astype(BF16)
    first = (1 - odd) * (leaves - CHILD)
    bulk1[pl.ds(0, CHILD * rank), :] = coef[blocks(first, CHILD, rank), :]
    bulk1[pl.ds(CHILD * rank, CHILD * leaf), :] = src[blocks(first, CHILD, leaf), :]
    loads[2 * PARTS].wait()
    loads[2 * PARTS + 1].wait()
    total = None
    for q in range(mids):
        mid = mm(up_leaf[q], coef[pl.ds(q * CHILD * rank, CHILD * rank), :]).astype(BF16)
        pack[pl.ds(q * rank, rank), :] = mid
        lift = mm(up_mid[q], mid).astype(BF16).astype(F32)
        total = lift if total is None else total + lift
    pack[pl.ds(mids * rank, rank), :] = total.astype(BF16)


def prepare(index, count, leaf_far, coef, src, work, bulk2):
    leaves = index.shape[1]
    slots = index.shape[0] // 2
    rank = coef.shape[0] // leaves
    leaf = src.shape[0] // (leaves + 1)
    device = lax.axis_index("leaf")
    odd = lax.rem(device, 2)
    core = lax.axis_index("col")
    base = odd * (leaves - CHILD)
    bulk2[pl.ds(0, CHILD * rank), :] = coef[blocks(base, CHILD, rank), :]
    bulk2[pl.ds(CHILD * rank, CHILD * leaf), :] = src[blocks(base, CHILD, leaf), :]
    lowest = jnp.where(odd == 1, leaves, -CHILD) + device * leaves


    def row(n, found):
        live = count[base + n]
        for f in range(FAR):
            at = leaf_far[f, base + n] - lowest
            work[7 + f, n] = jnp.where((at >= 0) & (at < CHILD), at, CHILD)
        out = []
        for r, owner in ((0, core), (1, 1 - core)):
            at = found[r]
            for k in range(slots):
                slot = owner * slots + k
                outside = index[slot, base + n] - lowest
                work[3 * r, at] = n * slots + k
                work[3 * r + 1, at] = outside
                work[3 * r + 2, at] = n
                use = (slot < live) & (outside >= 0) & (outside < CHILD)
                at = at + use.astype(jnp.int32)
            out.append(at)
        return tuple(out)

    found = lax.fori_loop(0, CHILD, row, (jnp.int32(0), jnp.int32(0)))
    rounds = (jnp.maximum(found[0], found[1]) + BATCH - 1) // BATCH
    work[6, 0] = rounds
    for r in range(2):

        def fill(n, _):
            work[3 * r, n] = 0
            work[3 * r + 1, n] = 0
            work[3 * r + 2, n] = CHILD
            return 0

        lax.fori_loop(found[r], rounds * BATCH, fill, 0)


def fold(group, after, basis_hbm, coupling_hbm, *refs):
    folded, basis, coupling, sems = refs[-4:]
    leaves, _, _ = basis_hbm.shape
    device = lax.axis_index("leaf")
    base = lax.rem(device, 2) * (leaves - CHILD)
    parent = device // group
    member = lax.rem(device, group)
    inner = (member > 0) & (member < group - 1)
    core = lax.axis_index("col")
    early = ((parent >= 2) | ((parent == 1) & inner)) & ((core == 0) | (parent >= 2))

    @pl.when(early != after)
    def _():
        loads = [
            pltpu.make_async_copy(a.at[pl.ds(base, CHILD)], b, sems.at[k])
            for k, (a, b) in enumerate(((basis_hbm, basis), (coupling_hbm, coupling)))
        ]
        for load in loads:
            load.start()
        for load in loads:
            load.wait()
        for n in range(CHILD):
            folded[n] = mm_t(basis[n], coupling[n]).astype(BF16)


def join(pack, pack1, pair, part):
    held = part.shape[0]
    mids = pack.shape[0] - held
    total = pack[pl.ds(mids, held), :].astype(F32) + pack1[pl.ds(mids, held), :].astype(F32)
    pair[pl.ds(0, mids), :] = pack[pl.ds(0, mids), :]
    pair[pl.ds(mids, mids), :] = pack1[pl.ds(0, mids), :]
    pair[pl.ds(2 * mids, held), :] = total.astype(BF16)
    part[...] = total.astype(BF16)


def cluster(pair, pair1, plane):
    mids = plane.shape[0] - pair.shape[0]
    held = pair.shape[0] - mids
    plane[pl.ds(0, mids), :] = pair[pl.ds(0, mids), :]
    plane[pl.ds(mids, mids), :] = pair1[pl.ds(0, mids), :]
    total = pair[pl.ds(mids, held), :].astype(F32) + pair1[pl.ds(mids, held), :].astype(F32)
    plane[pl.ds(2 * mids, held), :] = total.astype(BF16)


def stacked(*refs):
    out = refs[-1]
    held = refs[0].shape[0]
    for k, part in enumerate(refs[:-1]):
        out[pl.ds(k * held, held), :] = part[...]


def load_tiles(tiles_hbm, tiles, sems, base):
    loads = [
        pltpu.make_async_copy(tiles_hbm.at[base + n], tiles.at[n], sems.at[n])
        for n in range(tiles.shape[0])
    ]
    for load in loads:
        load.start()
    return loads


def product(index, live, held, n, k, slot, i, window, lowest, total):
    leaf = held.shape[3]
    at = index[slot, i] - lowest
    place = jnp.where((slot < live) & (at >= 0) & (at < total), at, total)
    return mm(held[n, k], window[blocks(place, 1, leaf), :])


def near_most(index, count, tiles_hbm, other, src, bulk1, acc1, acc2, tiles2, tiles1, window, sems1, sems2):
    leaves, slots, leaf, _ = other.shape
    device = lax.axis_index("leaf")
    odd = lax.rem(device, 2)
    core = lax.axis_index("col")
    base1 = (1 - odd) * (leaves - CHILD)
    base2 = odd * (leaves - CHILD)
    loads2 = load_tiles(tiles_hbm, tiles2, sems2, base2)
    loads1 = load_tiles(tiles_hbm, tiles1, sems1, base1)
    total = leaves + CHILD
    window[blocks(odd * CHILD, leaves, leaf), :] = src[pl.ds(0, leaves * leaf), :]
    window[blocks((1 - odd) * leaves, CHILD, leaf), :] = bulk1[pl.ds(bulk1.shape[0] - CHILD * leaf, CHILD * leaf), :]
    window[pl.ds(total * leaf, leaf), :] = jnp.zeros((leaf, src.shape[1]), BF16)
    lowest = device * leaves - odd * CHILD

    def others2(n, _):
        i = base2 + n
        acc2[blocks(n, 1, leaf), :] = sum(
            product(index, count[i], other, i, k, (1 - core) * slots + k, i, src, device * leaves, leaves)
            for k in range(slots)
        )
        return 0

    lax.fori_loop(0, CHILD, others2, 0, unroll=4)
    for load in loads2:
        load.wait()

    def own2(n, _):
        i = base2 + n
        acc2[blocks(n, 1, leaf), :] += sum(
            product(index, count[i], tiles2, n, k, core * slots + k, i, src, device * leaves, leaves)
            for k in range(slots)
        )
        return 0

    lax.fori_loop(0, CHILD, own2, 0, unroll=4)
    for load in loads1:
        load.wait()

    def all1(n, _):
        i = base1 + n
        acc1[blocks(n, 1, leaf), :] = sum(
            product(index, count[i], held, at, k, owner * slots + k, i, window, lowest, total)
            for held, at, owner in ((tiles1, n, core), (other, i, 1 - core))
            for k in range(slots)
        )
        return 0

    lax.fori_loop(0, CHILD, all1, 0, unroll=4)


def downward(
    leaf_far, mid_far,
    near1, near2, coef, bulk1, plane, next_a, next_b, beyond0, beyond1,
    basis, leaf_coupling, up_leaf, mid_coupling, up_mid, top_coupling,
    out, acc2,
    full, down, window, chosen, stack, sems,
):
    total_top = top_coupling.shape[0]
    leaves, rank, leaf = basis.shape
    mids = up_leaf.shape[0]
    group = CHILD // mids
    device = lax.axis_index("leaf")
    odd = lax.rem(device, 2)
    parent = device // group
    member = lax.rem(device, group)

    stack[blocks(parent, 1, rank), :] = jnp.zeros((rank, full.shape[1]), BF16)
    stack[blocks(jnp.bitwise_xor(parent, 1), 1, rank), :] = next_a[pl.ds(CHILD * rank, rank), :]
    for p in range(2, total_top):
        rows = pl.ds((p - 2) * rank, rank)
        top = beyond0[rows, :].astype(F32) + beyond1[rows, :].astype(F32)
        stack[blocks(jnp.bitwise_xor(parent, p), 1, rank), :] = top.astype(BF16)
    top_field = mm(top_coupling[parent], stack[...]).astype(BF16)

    total = leaves + CHILD
    lowest = device * leaves - odd * CHILD
    window[blocks(odd * CHILD, leaves, rank), :] = coef[...]
    window[blocks((1 - odd) * leaves, CHILD, rank), :] = bulk1[pl.ds(0, CHILD * rank), :]
    window[pl.ds(total * rank, rank), :] = jnp.zeros((rank, full.shape[1]), BF16)

    for q in range(mids):
        for f in range(FAR):
            b = mid_far[q, f]
            above = b // CHILD
            inside = lax.rem(b, CHILD)
            place = jnp.bitwise_xor(inside // mids, member) * mids + lax.rem(inside, mids)
            row = blocks(place, 1, rank)
            to = pl.ds((q * FAR + f) * rank, rank)
            beside = jnp.bitwise_xor(parent, 1)

            @pl.when(above == parent)
            def _():
                chosen[to, :] = plane[row, :]

            @pl.when(above == beside)
            def _():
                chosen[to, :] = next_a[row, :]

            @pl.when((above != parent) & (above != beside))
            def _():
                chosen[to, :] = next_b[row, :]

    for q in range(mids):
        picked = chosen[pl.ds(q * FAR * rank, FAR * rank), :]
        mid_field = (mm(mid_coupling[q], picked) + mm_t(up_mid[q], top_field)).astype(BF16)
        down[pl.ds(q * CHILD * rank, CHILD * rank), :] = mm_t(up_leaf[q], mid_field)

    def field_of(i):
        field = far_sum(leaf_far, leaf_coupling, window, i, lowest, total)
        return (field + down[blocks(i, 1, rank), :]).astype(BF16)

    base1 = (1 - odd) * (leaves - CHILD)
    base2 = odd * (leaves - CHILD)
    stores = []
    for n in range(CHILD):
        rows = pl.ds(n * leaf, leaf)
        full[rows, :] = near1[rows, :] + mm_t(basis[base1 + n], field_of(base1 + n))
        if n % 2 == 1:
            rows = pl.ds((n - 1) * leaf, 2 * leaf)
            stores.append(
                pltpu.make_async_copy(full.at[rows], out.at[blocks(base1 + n - 1, 2, leaf)], sems.at[n // 2])
            )
            stores[-1].start()
    for n in range(CHILD):
        rows = pl.ds(n * leaf, leaf)
        acc2[rows, :] = near2[rows, :] + mm_t(basis[base2 + n], field_of(base2 + n))
    for store in stores:
        store.wait()


def far_sum(leaf_far, leaf_coupling, window, i, lowest, total):
    rank = leaf_coupling.shape[1]
    picked = []
    for f in range(FAR):
        at = leaf_far[f, i] - lowest
        place = jnp.where((at >= 0) & (at < total), at, total)
        picked.append(window[blocks(place, 1, rank), :])
    return mm(leaf_coupling[i], jnp.concatenate(picked, axis=0))


def near_last(work, tiles, other, bulk2, acc_in, folded, out_in, out, acc, window, sems):
    leaves, slots, leaf, _ = other.shape
    rank = window.shape[0] // (CHILD + 1)
    odd = lax.rem(lax.axis_index("leaf"), 2)
    base = odd * (leaves - CHILD)
    window[pl.ds(0, CHILD * rank), :] = bulk2[pl.ds(0, CHILD * rank), :]
    window[pl.ds(CHILD * rank, rank), :] = jnp.zeros((rank, bulk2.shape[1]), BF16)
    skip = CHILD * rank

    def step(t, _):
        for b in range(BATCH):
            n = t * BATCH + b
            for r, held, low in ((0, tiles, 0), (1, other, base)):
                tile = work[3 * r, n]
                at = pl.multiple_of(skip + work[3 * r + 1, n] * leaf, rank)
                part = mm(held[low + tile // slots, lax.rem(tile, slots)], bulk2[pl.ds(at, leaf), :])
                acc[blocks(work[3 * r + 2, n], 1, leaf), :] += part
        return 0

    lax.fori_loop(0, work[6, 0], step, 0)
    stores = []
    for n in range(CHILD):
        rows = pl.ds(n * leaf, leaf)
        picked = [window[blocks(work[7 + f, n], 1, rank), :] for f in range(FAR)]
        acc[rows, :] += mm(folded[n], jnp.concatenate(picked, axis=0))
        stores.append(pltpu.make_async_copy(acc.at[rows], out.at[blocks(base + n, 1, leaf)], sems.at[n]))
        stores[-1].start()
    for store in stores:
        store.wait()


def shards(
    sources,
    near_tiles,
    near_index,
    near_count,
    leaf_basis,
    leaf_coupling,
    leaf_far,
    up_leaf,
    mid_coupling,
    mid_far,
    up_mid,
    top_coupling,
):
    sds = jax.ShapeDtypeStruct
    leaves, rank, leaf = leaf_basis.shape
    mids = up_leaf.shape[0]
    cols = sources.shape[1]
    slots = near_tiles.shape[1]
    total_top = top_coupling.shape[0]
    devices = lax.axis_size("leaf")
    group = CHILD // mids
    edge = CHILD * leaf
    edge_c = CHILD * rank
    rows = leaves * leaf
    assert leaves == 2 * CHILD and group == 4 and total_top >= 4
    product_flops = 2 * leaf * leaf * cols

    rest = [(i, i + 1) for i in range(1, devices - 1, 2)]
    rest = rest + [(j, i) for i, j in rest]

    def swap(k):
        return [(i, i ^ k) for i in range(devices)]

    def send(x, pairs, axis="leaf"):
        return lax.ppermute(x, axis, pairs)

    def call(kernel, out_shape, in_specs, out_specs, scratch, mib, estimate, **more):
        def run(*args):
            return pl.pallas_call(
                kernel,
                out_shape=out_shape,
                in_specs=in_specs,
                out_specs=out_specs,
                scratch_shapes=scratch,
                compiler_params=params(mib),
                cost_estimate=estimate,
                **more,
            )(*args)

        return run

    index, count, far_index, mid_index = map(in_hbm, (near_index.T, near_count, leaf_far.T, mid_far))
    own_tiles = in_hbm(near_tiles)

    pack, bulk1, coef, src = call(
        upward,
        (
            sds(((mids + 1) * rank, cols), BF16),
            sds((edge_c + edge, cols), BF16),
            sds((leaves * rank, cols), BF16),
            sds((rows + leaf, cols), BF16),
        ),
        [HBM] * 4,
        (VMEM,) * 4,
        [
            pltpu.VMEM(leaf_basis.shape, BF16),
            pltpu.VMEM(up_leaf.shape, BF16),
            pltpu.VMEM(up_mid.shape, BF16),
            pltpu.SemaphoreType.DMA((2 * PARTS + 2,)),
        ],
        8,
        cost(2 * leaves * rank * leaf * cols, 4 << 20),
    )(*map(in_hbm, (sources, leaf_basis, up_leaf, up_mid)))
    src = in_vmem(src)

    pack1 = send(pack, swap(1))
    bulk1 = send(bulk1, swap(1))
    other = in_vmem(send(near_tiles, [(0, 1), (1, 0)], "col"))

    work, bulk2 = call(
        prepare,
        (sds((7 + FAR, CHILD * slots + BATCH), jnp.int32), sds((edge_c + edge, cols), BF16)),
        [SMEM, SMEM, SMEM, VMEM, VMEM],
        (SMEM, VMEM),
        [],
        8,
        cost(0, 4 << 20),
    )(index, count, far_index, coef, src)

    held = mids * rank
    pair, part = call(
        join,
        (sds((2 * held + rank, cols), BF16), sds((rank, cols), BF16)),
        [VMEM] * 2,
        (VMEM,) * 2,
        [],
        4,
        cost(0, 1 << 18),
    )(pack, pack1)

    pair1 = send(pair, swap(2))
    parts = [send(part, swap(k * group)) for k in range(2, total_top)]
    plane = call(
        cluster,
        sds((4 * held + rank, cols), BF16),
        [VMEM] * 2,
        VMEM,
        [],
        4,
        cost(0, 1 << 18),
    )(pair, pair1)
    beyond = call(
        stacked,
        sds(((total_top - 2) * rank, cols), BF16),
        [VMEM] * len(parts),
        VMEM,
        [],
        4,
        cost(0, 1 << 18),
    )(*parts)
    next_pairs = [(i, i + group) for i in range(group, devices - group) if i % (2 * group) >= group]
    next_a = send(plane, swap(group))
    next_b = send(plane, next_pairs + [(j, i) for i, j in next_pairs])
    beyond1 = send(beyond, swap(2))
    bulk2 = send(bulk2, rest)

    folded = None
    for after in (False, True):
        held = [] if folded is None else [in_vmem(folded)]
        folded = call(
            functools.partial(fold, group, after),
            sds((CHILD, leaf, leaf_coupling.shape[2]), BF16),
            [HBM] * 2 + [VMEM] * len(held),
            VMEM,
            [
                pltpu.VMEM((CHILD,) + leaf_basis.shape[1:], BF16),
                pltpu.VMEM((CHILD,) + leaf_coupling.shape[1:], BF16),
                pltpu.SemaphoreType.DMA((2,)),
            ],
            6,
            cost(CHILD * 2 * leaf * leaf * rank, 2 << 20),
            **({"input_output_aliases": {2: 0}} if held else {}),
        )(in_hbm(leaf_basis), in_hbm(leaf_coupling), *held)

    half_tiles = (CHILD,) + near_tiles.shape[1:]
    near1, near2, tiles2 = call(
        near_most,
        (sds((edge, cols), F32), sds((edge, cols), F32), sds(half_tiles, BF16)),
        [SMEM, SMEM, HBM] + [VMEM] * 3,
        (VMEM,) * 3,
        [
            pltpu.VMEM(half_tiles, BF16),
            pltpu.VMEM((rows + edge + leaf, cols), BF16),
            pltpu.SemaphoreType.DMA((CHILD,)),
            pltpu.SemaphoreType.DMA((CHILD,)),
        ],
        20,
        cost(leaves * 2 * slots * product_flops, 16 << 20),
    )(index, count, own_tiles, other, src, bulk1)

    out, acc2 = call(
        downward,
        (sds((rows, cols), F32), sds((edge + leaf, cols), F32)),
        [SMEM] * 2 + [VMEM] * 15,
        (ANY, VMEM),
        [
            pltpu.VMEM((edge, cols), F32),
            pltpu.VMEM((leaves * rank, cols), F32),
            pltpu.VMEM((edge_c + (leaves + 1) * rank, cols), BF16),
            pltpu.VMEM((mids * FAR * rank, cols), BF16),
            pltpu.VMEM((total_top * rank, cols), BF16),
            pltpu.SemaphoreType.DMA((CHILD // 2,)),
        ],
        16,
        cost(leaves * 4 * product_flops, 12 << 20),
    )(
        far_index, mid_index,
        near1, near2, coef, bulk1, plane, next_a, next_b, beyond, beyond1,
        leaf_basis, leaf_coupling, up_leaf, mid_coupling, up_mid, top_coupling,
    )

    product, _ = call(
        near_last,
        (sds((rows, cols), F32), sds((edge + leaf, cols), F32)),
        [SMEM] + [VMEM] * 5 + [ANY],
        (ANY, VMEM),
        [pltpu.VMEM((edge_c + rank, cols), BF16), pltpu.SemaphoreType.DMA((CHILD,))],
        8,
        cost(leaves * slots * product_flops, 4 << 20),
        input_output_aliases={6: 0, 4: 1},
    )(work, in_vmem(tiles2), other, bulk2, in_vmem(acc2), folded, out)
    return product


def solution(mesh):


    return jax.shard_map(
        shards,
        mesh=mesh,
        in_specs=(
            P("leaf", "col"),
            P("leaf", "col", None, None),
            P("leaf", None),
            P("leaf"),
            P("leaf", None, None),
            P("leaf", None, None),
            P("leaf", None),
            P("leaf", None, None),
            P("leaf", None, None),
            P("leaf", None),
            P("leaf", None, None),
            P(),
        ),
        out_specs=P("leaf", "col"),
        check_vma=False,
    )
```
